256 devices in a mesh: row: 32 (over z, x), col: 8 (over y, core).
Axes of the slice: x: 4, y: 4, z: 8, core: 2. Of those that a mesh axis runs over, the one named last changes fastest.
Arguments:
- displacement: float32 [3, 256, 4, 128], P(None, ('row', 'col')), may hold values from -6 to 6
- load: float32 [3, 256, 4, 128], P(None, ('row', 'col')), may hold values from -6 to 6
- elastic_tangent: bfloat16 [21, 8, 256, 4, 128], P(None, None, ('row', 'col')), may hold values from -4 to 4
- band_flags: int32 [8, 256, 4, 128], P(None, ('row', 'col')), may hold values from 0 to 1, as said below
- contact_stiffness: bfloat16 [8192, 8, 2048], P(('row', 'col')), may hold values from 0.29882812 to 3
- normals: float32 [3, 8, 2048], replicated, as said below
- branch_length: float32 [8, 2048], replicated, may hold values from 0.5 to 2
- neighbours: int32 [8, 2048], replicated, may hold values from 0 to 2047, as said below
Outputs:
- residual: float32 [3, 256, 4, 128], P(None, ('row', 'col'))
- stress: float32 [6, 8, 256, 4, 128], P(None, None, ('row', 'col'))
- band_tangent: float32 [21, 8192], P(None, ('row', 'col'))
- band_stress: float32 [6, 8192], P(None, ('row', 'col'))
The draws below stay inside these ranges and needn't reach their ends.
Inputs may be any that keep to these rules, and one draw needn't show every extreme that they name: `band_flags`: each block of 1 x-planes holds at most 32 flagged points, some blocks exactly 32; slots of contact_stiffness past a block's count are unused. `normals`: unit vectors. `neighbours`: every grain names at least 4 other grains; unused contact slots name the grain itself.
All inputs are finite; a program needn't handle non-finite values.
Results may differ from the reference program's by a relative error of at most 0.0003.
Values sent between devices are 32-bit elements; how exact they have to be, the bound alone decides.
No kernel may reach another device: no remote copies, remote signals or barrier semaphores. Data moves between devices by JAX's collectives and lax.ppermute only.
A program may use at most 128 MiB of HBM per device.

```python
import math
import jax
import jax.numpy as jnp
import numpy as np
from jax import lax

EX = 1
NY = 4
NZ = 128
GRAINS = 2048
CONTACTS = 8
SWEEPS = 4
BAND_MAX = 32
NX = 256
SLOTS = 8192
N_ROW = 32
N_COL = 8


def draw_normals(key, part):
    key_theta, key_phi = jax.random.split(key)
    theta = jax.random.uniform(key_theta, (CONTACTS, GRAINS), jnp.float32, 0.15, math.pi - 0.15)
    phi = jax.random.uniform(key_phi, (CONTACTS, GRAINS), jnp.float32, -math.pi, math.pi)
    return jnp.stack([jnp.sin(theta) * jnp.cos(phi), jnp.sin(theta) * jnp.sin(phi), jnp.cos(theta)]).astype(jnp.float32)


def draw_neighbours(key, part):
    key_count, key_step, key_sign = jax.random.split(key, 3)
    counts = jax.random.randint(key_count, (GRAINS,), 4, CONTACTS + 1)
    strides = jax.random.randint(key_step, (CONTACTS, GRAINS), 1, 64)
    signs = jax.random.randint(key_sign, (CONTACTS, GRAINS), 0, 2) * 2 - 1
    grain_ids = jnp.arange(GRAINS, dtype=jnp.int32)
    target = (grain_ids[None, :] + signs * strides) % GRAINS
    slot_ids = jnp.arange(CONTACTS, dtype=jnp.int32)[:, None]
    return jnp.where(slot_ids < counts[None, :], target, grain_ids[None, :]).astype(jnp.int32)


def permute_points(one_key):
    return jax.random.permutation(one_key, 8 * EX * NY * NZ)


def draw_band_flags(key, part):
    blocks = NX // EX
    key_start, key_cold, key_perm = jax.random.split(key, 3)
    start = jax.random.randint(key_start, (), 0, blocks)
    block_ids = jnp.arange(blocks, dtype=jnp.int32)
    hot_block = (block_ids - start) % blocks < max(1, blocks // 5)
    cold = jax.random.randint(key_cold, (blocks,), BAND_MAX // 4, BAND_MAX // 2 + 1)
    counts = jnp.where(hot_block, BAND_MAX, cold)
    ranks = jax.vmap(permute_points)(jax.random.split(key_perm, blocks))
    flags = (ranks < counts[:, None]).astype(jnp.int32)
    return flags.reshape(blocks, 8, EX, NY, NZ).transpose(1, 0, 2, 3, 4).reshape(8, NX, NY, NZ)


def level_of(rng, extent, cuts, least, high):
    loudness, own = 1.0, jax.random.fold_in(rng, 6)
    for dim, parts in cuts:
        heights = jnp.exp(jax.random.uniform(jax.random.fold_in(own, dim), (parts,), jnp.float32, least / len(cuts), high / len(cuts)))
        loudness = loudness * jnp.repeat(heights, extent[dim] // parts).reshape([-1 if axis == dim else 1 for axis in range(len(extent))])
    return loudness


def bell_draw(own_key, shape, spread, reach, cuts=(), kind=jnp.bfloat16):
    array = jax.random.normal(own_key, shape, jnp.float32) * spread
    if len(cuts) > 0:
        array = level_of(own_key, shape, cuts, -0.22, 0.18) * array
    return jnp.clip(array, min=-reach, max=reach).astype(kind)


def setup_inputs(seed: int = 0) -> dict:
    keys = jax.random.split(jax.random.key(seed), 9)
    return {
        "displacement": bell_draw(keys[0], (3, NX, NY, NZ), 1.0, 6.0, ((1, 256),), jnp.float32),
        "load": bell_draw(keys[1], (3, NX, NY, NZ), 1.0, 6.0, ((1, 256),), jnp.float32),
        "elastic_tangent": bell_draw(keys[2], (21, 8, NX, NY, NZ), 0.3, 4.0, ((2, 256),)),
        "band_flags": draw_band_flags(jax.random.fold_in(keys[8], 71), 0),
        "contact_stiffness": jnp.clip(jnp.exp(math.log(3.0) - 2.306499 * jax.random.uniform(keys[4], (SLOTS, CONTACTS, GRAINS), jnp.float32) ** level_of(keys[4], (SLOTS, CONTACTS, GRAINS), ((0, 256),), -0.2, 0.2)), 0.29882812, 3.0).astype(jnp.bfloat16),
        "normals": draw_normals(jax.random.fold_in(keys[8], 71), 0),
        "branch_length": jnp.clip(jnp.exp(jax.random.uniform(keys[6], (CONTACTS, GRAINS), jnp.float32, math.log(0.5), math.log(2.0))), 0.5, 2.0),
        "neighbours": draw_neighbours(jax.random.fold_in(keys[8], 71), 0),
    }


RELAX_FACTOR = 0.8

def shape_table():
    low_point = 0.5 - 0.5 / np.sqrt(3.0)
    high_point = 0.5 + 0.5 / np.sqrt(3.0)
    deriv_table = np.zeros((8, 8, 3))
    for corner in range(8):
        corner_bits = [corner >> 2 & 1, corner >> 1 & 1, corner & 1]
        for gauss_id in range(8):
            gauss_bits = [gauss_id >> 2 & 1, gauss_id >> 1 & 1, gauss_id & 1]
            coords = [high_point if flag_bit else low_point for flag_bit in gauss_bits]
            values = [coords[axis_id] if corner_bits[axis_id] else 1.0 - coords[axis_id] for axis_id in range(3)]
            slopes = [1.0 if corner_bits[axis_id] else -1.0 for axis_id in range(3)]
            for axis_id in range(3):
                product = slopes[axis_id]
                for other_axis in range(3):
                    if other_axis != axis_id:
                        product = product * values[other_axis]
                deriv_table[corner, gauss_id, axis_id] = product
    return jnp.asarray(deriv_table, jnp.float32)

def pair_list():
    return [(row_id, col_id) for row_id in range(6) for col_id in range(row_id, 6)]

def corner_values(padded, size_x, size_y, size_z):
    pieces = []
    for corner in range(8):
        shift_x, shift_y, shift_z = (corner >> 2 & 1, corner >> 1 & 1, corner & 1)
        pieces.append(padded[:, shift_x:shift_x + size_x, shift_y:shift_y + size_y, shift_z:shift_z + size_z])
    return jnp.stack(pieces, axis=1)

def gauss_strains(corners):
    gradient = jnp.einsum('iaxyz,agj->ijgxyz', corners, shape_table(), precision=lax.Precision.HIGHEST)
    return jnp.stack([gradient[0, 0], gradient[1, 1], gradient[2, 2], gradient[1, 2] + gradient[2, 1], gradient[0, 2] + gradient[2, 0], gradient[0, 1] + gradient[1, 0]])

def elastic_stress(packed, strain):
    pairs = pair_list()
    result_rows = []
    for row_id in range(6):
        running = jnp.zeros_like(strain[0])
        for col_id in range(6):
            position = pairs.index((min(row_id, col_id), max(row_id, col_id)))
            running = running + packed[position].astype(jnp.float32) * strain[col_id]
        result_rows.append(running)
    return jnp.stack(result_rows)

def nodal_forces(stress):
    voigt_rows = [[0, 5, 4], [5, 1, 3], [4, 3, 2]]
    tensor = jnp.stack([jnp.stack([stress[comp_id] for comp_id in row_list]) for row_list in voigt_rows])
    return 0.125 * jnp.einsum('ijgxyz,agj->iaxyz', tensor, shape_table(), precision=lax.Precision.HIGHEST)

def assemble(corner_forces):
    summed = None
    for corner in range(8):
        shift_x, shift_y, shift_z = (corner >> 2 & 1, corner >> 1 & 1, corner & 1)
        placed = jnp.pad(corner_forces[:, corner], ((0, 0), (shift_x, 1 - shift_x), (shift_y, 1 - shift_y), (shift_z, 1 - shift_z)))
        summed = placed if summed is None else summed + placed
    return summed

def contact_template(normals, neighbours):
    grain_total = neighbours.shape[1]
    contact_mask = (neighbours != jnp.arange(grain_total, dtype=jnp.int32)[None, :]).astype(jnp.float32)
    projector = jnp.stack([normals[0] * normals[0], normals[1] * normals[1], normals[2] * normals[2], normals[1] * normals[2], normals[0] * normals[2], normals[0] * normals[1]])
    return (contact_mask, projector)

def relax_rve(strain_row, stiffness, normals, branch_length, neighbours, contact_mask, projector):
    grain_total = neighbours.shape[1]
    weights = stiffness.astype(jnp.float32) * contact_mask
    affine = branch_length * lax.optimization_barrier(jnp.sum(strain_row[:, None, None] * projector, axis=0))
    diagonal = lax.optimization_barrier(jnp.sum(weights, axis=0))
    fluctuation = jnp.zeros((3, grain_total), jnp.float32)
    for sweep_id in range(SWEEPS):
        stretch = affine + lax.optimization_barrier(jnp.sum(normals * (fluctuation[:, neighbours] - fluctuation[:, None, :]), axis=0))
        unbalanced = lax.optimization_barrier(jnp.sum(normals * (weights * stretch)[None], axis=1))
        fluctuation = fluctuation + RELAX_FACTOR * unbalanced / diagonal[None, :]
    stretch = affine + lax.optimization_barrier(jnp.sum(normals * (fluctuation[:, neighbours] - fluctuation[:, None, :]), axis=0))
    contact_force = (weights * stretch * branch_length).reshape(-1)
    flat_proj = projector.reshape(6, -1)
    stress_row = jnp.dot(flat_proj, contact_force, precision=lax.Precision.HIGHEST) / grain_total
    stiff_term = (weights * branch_length * branch_length).reshape(-1)
    full = jnp.dot(flat_proj * stiff_term[None, :], flat_proj.T, precision=lax.Precision.HIGHEST) / grain_total
    tangent_row = jnp.stack([full[row_id, col_id] for row_id, col_id in pair_list()])
    return (stress_row, tangent_row)

def reference(displacement, load, elastic_tangent, band_flags, contact_stiffness, normals, branch_length, neighbours):
    devices = N_ROW * N_COL
    padded = jnp.pad(displacement, ((0, 0), (0, 1), (0, 1), (0, 1)))
    strain = gauss_strains(corner_values(padded, NX, NY, NZ))
    elastic = elastic_stress(elastic_tangent, strain)
    points = 8 * EX * NY * NZ
    strain_dev = strain.reshape(6, 8, devices, EX, NY, NZ).transpose(2, 0, 1, 3, 4, 5).reshape(devices, 6, points)
    flags_dev = band_flags.reshape(8, devices, EX, NY, NZ).transpose(1, 0, 2, 3, 4).reshape(devices, points)
    stiff_dev = contact_stiffness.reshape(devices, BAND_MAX, CONTACTS, GRAINS)
    contact_mask, projector = contact_template(normals, neighbours)

    def relax_slot(strain_row, stiffness):
        return relax_rve(strain_row, stiffness, normals, branch_length, neighbours, contact_mask, projector)

    def per_device(inputs):
        strain_one, flags_one, stiff_one = inputs
        flag_rank = jnp.cumsum(flags_one) - 1
        slot_ids = jnp.arange(BAND_MAX, dtype=jnp.int32)
        select = ((flag_rank[None, :] == slot_ids[:, None]) & (flags_one[None, :] == 1)).astype(jnp.float32)
        slot_strain = jnp.dot(select, strain_one.T, precision=lax.Precision.HIGHEST)
        live_count = jnp.sum(flags_one)
        slot_stress, slot_tangent = jax.vmap(relax_slot)(slot_strain, stiff_one)
        live = (slot_ids < live_count)[:, None]
        slot_stress = jnp.where(live, slot_stress, 0.0)
        slot_tangent = jnp.where(live, slot_tangent, 0.0)
        band_part = jnp.dot(slot_stress.T, select, precision=lax.Precision.HIGHEST)
        return (band_part, slot_tangent, slot_stress)
    band_part, tangents, slot_stresses = lax.map(per_device, (strain_dev, flags_dev, stiff_dev))
    band_full = band_part.reshape(devices, 6, 8, EX, NY, NZ).transpose(1, 2, 0, 3, 4, 5).reshape(6, 8, NX, NY, NZ)
    stress = jnp.where(band_flags[None] == 1, band_full, elastic)
    summed = assemble(nodal_forces(stress))
    residual = load - summed[:, :NX, :NY, :NZ]
    band_tangent = tangents.reshape(devices * BAND_MAX, 21).T
    band_stress = slot_stresses.reshape(devices * BAND_MAX, 6).T
    return (residual, stress, band_tangent, band_stress)
```

```python
import jax
import jax.numpy as jnp
import numpy as np
from jax import lax
from jax.experimental import pallas as pl
from jax.experimental.pallas import tpu as pltpu
from jax.sharding import PartitionSpec as P

SWEEPS = 4
RELAX_FACTOR = 0.8
LOW = float(0.5 - 0.5 / np.sqrt(3.0))
HIGH = float(0.5 + 0.5 / np.sqrt(3.0))
GRAINS = 2048
CONTACTS = 8
SLOT_COUNT = 32
GROUPS = SLOT_COUNT // 8
CHUNKS = GRAINS // 128
PAIRS = [(row_id, col_id) for row_id in range(6) for col_id in range(row_id, 6)]
NT = (((1,), (1,)), ((), ()))


def shifted(value, axis, steps):
    count = lax.axis_size(axis)
    leading, last = (max(0, -steps), min(count, count - steps))
    return lax.ppermute(value, axis, [(source, source + steps) for source in range(leading, last)])


def lanes_of(chunk):
    return pl.ds(pl.multiple_of(chunk * 128, 128), 128)


def row8(ref, row, lanes):
    return jnp.broadcast_to(ref[row : row + 1, lanes], (8, 128))


def take_lanes(table, index):
    return jnp.take_along_axis(table, index, axis=1, mode="promise_in_bounds")


def template_kernel(
    flags_ref,
    stiff_ref,
    nrm_ref,
    br_ref,
    nbr_ref,
    wt_ref,
    cd_ref,
    tan_ref,
    rank_ref,
    sel_ref,
    lp_ref,
    near_ref,
    raw_ref,
    basis_ref,
    high_ref,
    low_ref,
):
    flags = flags_ref[...]
    flags_f = flags.astype(jnp.float32)
    tri = (
        lax.broadcasted_iota(jnp.int32, (128, 128), 0)
        <= lax.broadcasted_iota(jnp.int32, (128, 128), 1)
    ).astype(jnp.float32)
    inside = jnp.dot(flags_f, tri, preferred_element_type=jnp.float32)
    before = (
        lax.broadcasted_iota(jnp.int32, (32, 32), 1) < lax.broadcasted_iota(jnp.int32, (32, 32), 0)
    ).astype(jnp.float32)
    ahead = jnp.sum(
        jnp.dot(before, flags_f, preferred_element_type=jnp.float32), axis=1, keepdims=True
    )
    rank = jnp.where(flags == 1, (inside + ahead - 1.0).astype(jnp.int32), -1)
    rank_ref[...] = rank
    live_total = jnp.sum(flags_f)
    slot_rows = lax.broadcasted_iota(jnp.int32, (32, 128), 0)
    for row in range(32):
        picked = jnp.broadcast_to(rank_ref[row : row + 1, :], (32, 128)) == slot_rows
        sel_ref[:, row * 128 : (row + 1) * 128] = jnp.where(picked, 1.0, 0.0).astype(jnp.bfloat16)

    basis_ref[168:256, :] = jnp.zeros((88, 128), jnp.float32)
    for chunk in range(CHUNKS):
        lanes = slice(chunk * 128, (chunk + 1) * 128)
        names = nbr_ref[:, lanes]
        own = lax.broadcasted_iota(jnp.int32, (8, 128), 1) + chunk * 128
        reach = (names - (chunk * 128 - 64)) & (GRAINS - 1)
        widest = jnp.max(reach.astype(jnp.float32))
        near_ref[chunk] = (widest < 256.0).astype(jnp.int32)

    def chunk_step(chunk, carry):
        lanes = lanes_of(chunk)
        names = nbr_ref[:, lanes]
        own = lax.broadcasted_iota(jnp.int32, (8, 128), 1) + chunk * 128
        mask = jnp.where(names != own, 1.0, 0.0)
        n0, n1, n2 = (nrm_ref[axis_id, :, lanes] for axis_id in range(3))
        length = br_ref[:, lanes]
        proj = [n0 * n0, n1 * n1, n2 * n2, n1 * n2, n0 * n2, n0 * n1]
        scaled = [length * value for value in proj]
        for comp in range(6):
            lp_ref[comp, :, lanes] = scaled[comp]
        for place, (row_id, col_id) in enumerate(PAIRS):
            basis_ref[place * 8 : (place + 1) * 8, :] = scaled[row_id] * scaled[col_id]
        for contact in range(CONTACTS):
            basis = basis_ref[pl.ds(contact, 32, stride=8), :]
            high = basis.astype(jnp.bfloat16)
            high_ref[contact, :, lanes] = high
            low_ref[contact, :, lanes] = (basis - high.astype(jnp.float32)).astype(jnp.bfloat16)
        for slot in range(SLOT_COUNT):
            raw_ref[slot * 8 : (slot + 1) * 8, :] = (
                stiff_ref[slot, :, lanes].astype(jnp.float32) * mask
            )
        for group in range(GROUPS):
            total = None
            for contact in range(CONTACTS):
                value = raw_ref[pl.ds(group * 64 + contact, 8, stride=8), :]
                wt_ref[contact, group * 8 : (group + 1) * 8, lanes] = value
                total = value if total is None else total + value
            cd_ref[group * 8 : (group + 1) * 8, lanes] = RELAX_FACTOR / total
        return carry

    lax.fori_loop(0, CHUNKS, chunk_step, 0)

    acc = jnp.zeros((32, 32), jnp.float32)
    for contact in range(CONTACTS):
        weights = wt_ref[contact].astype(jnp.bfloat16)
        for part_ref in (high_ref, low_ref):
            acc = acc + lax.dot_general(
                part_ref[contact], weights, NT, preferred_element_type=jnp.float32
            )
    slot_lane = lax.broadcasted_iota(jnp.int32, (32, 32), 1).astype(jnp.float32)
    acc = jnp.where(slot_lane < live_total, acc * (1.0 / GRAINS), 0.0)
    tan_ref[...] = acc[:21]


def lerp(low_value, high_value, bit):
    weight = HIGH if bit else LOW
    return low_value + weight * (high_value - low_value)


def strain_rows(plane_refs, dup_ref):
    row = lax.broadcasted_iota(jnp.int32, (8, 128), 0)
    lane = lax.broadcasted_iota(jnp.int32, (8, 128), 1)
    z_weight = jnp.where(row < 4, LOW, HIGH)
    last_y = (row & 3) == 3
    last_z = lane == 127
    gradient = {}
    for axis_id in range(3):
        along, slope = {}, {}
        for bit_x in range(2):
            plane = plane_refs[bit_x][axis_id]
            dup_ref[0:4, :] = plane
            dup_ref[4:8, :] = plane
            base = dup_ref[...]
            for bit_y in range(2):
                value = base if bit_y == 0 else jnp.where(last_y, 0.0, pltpu.roll(base, 7, 0))
                after = jnp.where(last_z, 0.0, pltpu.roll(value, 127, 1))
                slope[bit_x, bit_y] = after - value
                along[bit_x, bit_y] = value + z_weight * (after - value)
        for gauss_y in range(2):
            for gauss_x in range(2):
                point = 2 * gauss_x + gauss_y
                face = [lerp(along[bit_x, 0], along[bit_x, 1], gauss_y) for bit_x in range(2)]
                gradient[point, axis_id, 0] = face[1] - face[0]
                gradient[point, axis_id, 1] = lerp(
                    along[0, 1] - along[0, 0], along[1, 1] - along[1, 0], gauss_x
                )
                edge = [lerp(slope[bit_x, 0], slope[bit_x, 1], gauss_y) for bit_x in range(2)]
                gradient[point, axis_id, 2] = lerp(edge[0], edge[1], gauss_x)
    return [
        [
            gradient[point, 0, 0],
            gradient[point, 1, 1],
            gradient[point, 2, 2],
            gradient[point, 1, 2] + gradient[point, 2, 1],
            gradient[point, 0, 2] + gradient[point, 2, 0],
            gradient[point, 0, 1] + gradient[point, 1, 0],
        ]
        for point in range(4)
    ]


def weigh(low_value, high_value, corner_bit):
    if corner_bit:
        return LOW * low_value + HIGH * high_value
    return HIGH * low_value + LOW * high_value


def force_rows(stress):
    row = lax.broadcasted_iota(jnp.int32, (8, 128), 0)
    lane = lax.broadcasted_iota(jnp.int32, (8, 128), 1)
    z_high = jnp.where(row < 4, LOW, HIGH)
    z_low = jnp.where(row < 4, HIGH, LOW)
    voigt = [[0, 5, 4], [5, 1, 3], [4, 3, 2]]
    planes = [[None] * 3, [None] * 3]
    for axis_id in range(3):
        part = [[stress[point][voigt[axis_id][other]] for point in range(4)] for other in range(3)]
        flow = [part[0][gauss_y] + part[0][2 + gauss_y] for gauss_y in range(2)]
        for bit_x in range(2):
            side_y = [weigh(part[1][gauss_y], part[1][2 + gauss_y], bit_x) for gauss_y in range(2)]
            side_z = [weigh(part[2][gauss_y], part[2][2 + gauss_y], bit_x) for gauss_y in range(2)]
            total_y = side_y[0] + side_y[1]
            total = None
            for bit_y in range(2):
                first = weigh(flow[0], flow[1], bit_y)
                first = first if bit_x else -first
                first = first + total_y if bit_y else first - total_y
                second = weigh(side_z[0], side_z[1], bit_y)
                near = z_low * first - second
                far = z_high * first + second
                far = jnp.where(lane == 0, 0.0, pltpu.roll(far, 1, 1))
                both = near + far
                both = both + pltpu.roll(both, 4, 0)
                if bit_y:
                    both = jnp.where((row & 3) == 0, 0.0, pltpu.roll(both, 1, 0))
                total = both if total is None else total + both
            planes[bit_x][axis_id] = 0.125 * total
    return planes


def relax_kernel(
    near_ref,
    disp_ref,
    upper_ref,
    load_ref,
    tangent_ref,
    rank_ref,
    sel_ref,
    wt_ref,
    cd_ref,
    lp_ref,
    nrm_ref,
    nbr_ref,
    pre_ref,
    carried_ref,
    stress_ref,
    band_ref,
    dup_ref,
    strain_ref,
    split_high_ref,
    split_low_ref,
    affine_ref,
    fluct_ref,
    sums_ref,
    far_ref,
):
    tiles = strain_rows((disp_ref, upper_ref), dup_ref)
    for point in range(4):
        for comp in range(6):
            start = comp * 32 + point * 8
            strain_ref[start : start + 8, :] = tiles[point][comp]
    strain_ref[192:256, :] = jnp.zeros((64, 128), jnp.float32)

    for row in range(32):
        value = strain_ref[pl.ds(row, 8, stride=32), :]
        high = value.astype(jnp.bfloat16)
        split_high_ref[:, row * 128 : (row + 1) * 128] = high
        split_low_ref[:, row * 128 : (row + 1) * 128] = (value - high.astype(jnp.float32)).astype(
            jnp.bfloat16
        )
    sel = sel_ref[...]
    slot_strain = lax.dot_general(
        sel, split_high_ref[...], NT, preferred_element_type=jnp.float32
    ) + lax.dot_general(sel, split_low_ref[...], NT, preferred_element_type=jnp.float32)
    columns = [
        [
            jnp.broadcast_to(slot_strain[group * 8 : (group + 1) * 8, comp : comp + 1], (8, 128))
            for comp in range(6)
        ]
        for group in range(GROUPS)
    ]
    sums_ref[...] = jnp.zeros((192, 128), jnp.float32)

    def first_step(chunk, carry):
        lanes = lanes_of(chunk)
        totals = [[None] * 3 for _ in range(GROUPS)]
        for contact in range(CONTACTS):
            basis = [row8(lp_ref.at[comp], contact, lanes) for comp in range(6)]
            normal = [row8(nrm_ref.at[axis_id], contact, lanes) for axis_id in range(3)]
            for group in range(GROUPS):
                rows = slice(group * 8, (group + 1) * 8)
                affine = columns[group][0] * basis[0]
                for comp in range(1, 6):
                    affine = affine + columns[group][comp] * basis[comp]
                affine_ref[contact, rows, lanes] = affine
                force = wt_ref[contact, rows, lanes] * affine
                for axis_id in range(3):
                    term = force * normal[axis_id]
                    old = totals[group][axis_id]
                    totals[group][axis_id] = term if old is None else old + term
        for group in range(GROUPS):
            rows = slice(group * 8, (group + 1) * 8)
            factor = cd_ref[rows, lanes]
            for axis_id in range(3):
                start = axis_id * 32 + group * 8
                fluct_ref[0, start : start + 8, lanes] = factor * totals[group][axis_id]
        return carry

    lax.fori_loop(0, CHUNKS, first_step, 0)

    half = lax.broadcasted_iota(jnp.int32, (8, 128), 1) < 64

    def chunk_work(source, chunk, finish, near):
        lanes = lanes_of(chunk)
        lanes_up = lanes_of((chunk + 1) & (CHUNKS - 1))
        lanes_down = lanes_of((chunk + CHUNKS - 1) & (CHUNKS - 1))
        for group in range(GROUPS):
            rows = slice(group * 8, (group + 1) * 8)
            starts = [axis_id * 32 + group * 8 for axis_id in range(3)]
            own = [fluct_ref[source, start : start + 8, lanes] for start in starts]
            if near:
                sides = [
                    jnp.where(
                        half,
                        fluct_ref[source, start : start + 8, lanes_up],
                        fluct_ref[source, start : start + 8, lanes_down],
                    )
                    for start in starts
                ]
            stretches = []
            for contact in range(CONTACTS):
                normal = [row8(nrm_ref.at[axis_id], contact, lanes) for axis_id in range(3)]
                if near:
                    names = row8(nbr_ref, contact, lanes)
                    index = names & 127
                    inside = (names >> 7) == chunk
                    moved = [
                        jnp.where(
                            inside,
                            take_lanes(own[axis_id], index),
                            take_lanes(sides[axis_id], index),
                        )
                        for axis_id in range(3)
                    ]
                else:
                    moved = [far_ref[contact, start : start + 8, :] for start in starts]
                stretch = affine_ref[contact, rows, lanes]
                for axis_id in range(3):
                    stretch = stretch + normal[axis_id] * (moved[axis_id] - own[axis_id])
                force = wt_ref[contact, rows, lanes] * stretch
                stretches.append((force, normal))
            finish(group, rows, lanes, own, stretches)

    def gather_far(source, chunk):
        lanes = lanes_of(chunk)
        for contact in range(CONTACTS):
            names = row8(nbr_ref, contact, lanes)
            index = names & 127
            block = names >> 7

            def step(place, values):
                hit = block == place
                return tuple(
                    jnp.where(
                        hit,
                        take_lanes(
                            fluct_ref[source, tile * 8 : (tile + 1) * 8, lanes_of(place)], index
                        ),
                        values[tile],
                    )
                    for tile in range(12)
                )

            zero = jnp.zeros((8, 128), jnp.float32)
            values = lax.fori_loop(0, CHUNKS, step, (zero,) * 12)
            for tile in range(12):
                far_ref[contact, tile * 8 : (tile + 1) * 8, :] = values[tile]

    def both_ways(source, chunk, finish):
        near = near_ref[chunk] == 1

        @pl.when(near)
        def _():
            chunk_work(source, chunk, finish, True)

        @pl.when(jnp.logical_not(near))
        def _():
            gather_far(source, chunk)
            chunk_work(source, chunk, finish, False)

    def sweep_step(turn, carry):
        source = turn & 1
        target = 1 - source

        def finish(group, rows, lanes, own, stretches):
            factor = cd_ref[rows, lanes]
            for axis_id in range(3):
                total = None
                for force, normal in stretches:
                    term = force * normal[axis_id]
                    total = term if total is None else total + term
                start = axis_id * 32 + group * 8
                fluct_ref[target, start : start + 8, lanes] = own[axis_id] + factor * total

        def step(chunk, inner):
            both_ways(source, chunk, finish)
            return inner

        return lax.fori_loop(0, CHUNKS, step, carry)

    lax.fori_loop(0, SWEEPS - 1, sweep_step, 0)

    def finish_stress(group, rows, lanes, own, stretches):
        for comp in range(6):
            start = comp * 32 + group * 8
            total = sums_ref[start : start + 8, :]
            for contact in range(CONTACTS):
                total = total + stretches[contact][0] * row8(lp_ref.at[comp], contact, lanes)
            sums_ref[start : start + 8, :] = total

    def last_step(chunk, carry):
        both_ways((SWEEPS - 1) & 1, chunk, finish_stress)
        return carry

    lax.fori_loop(0, CHUNKS, last_step, 0)

    lane32 = lax.broadcasted_iota(jnp.int32, (32, 128), 1)
    table = jnp.zeros((32, 128), jnp.float32)
    for comp in range(6):
        total = jnp.sum(sums_ref[comp * 32 : (comp + 1) * 32, :], axis=1, keepdims=True)
        table = jnp.where(lane32 == comp, total * (1.0 / GRAINS), table)
    full = jnp.concatenate([table, jnp.zeros((96, 128), jnp.float32)], axis=0)
    flipped = jnp.transpose(full)
    band_ref[...] = flipped[0:6, 0:32]
    dup_ref[...] = flipped[0:8, :]

    strain = [strain_ref[comp * 32 : (comp + 1) * 32, :] for comp in range(6)]
    rank = rank_ref[...]
    banded = rank >= 0
    place = jnp.maximum(rank, 0)
    stress = []
    for row_id in range(6):
        running = None
        for col_id in range(6):
            where = PAIRS.index((min(row_id, col_id), max(row_id, col_id)))
            term = (
                tangent_ref[where * 32 : (where + 1) * 32, :].astype(jnp.float32) * strain[col_id]
            )
            running = term if running is None else running + term
        values = take_lanes(jnp.broadcast_to(dup_ref[row_id : row_id + 1, :], (32, 128)), place)
        value = jnp.where(banded, values, running)
        stress_ref[row_id * 32 : (row_id + 1) * 32, :] = value
        stress.append(value)
    planes = force_rows(
        [[stress[comp][point * 8 : (point + 1) * 8, :] for comp in range(6)] for point in range(4)]
    )
    for axis_id in range(3):
        pre_ref[axis_id] = load_ref[axis_id] - planes[0][axis_id][0:4]
        carried_ref[axis_id] = planes[1][axis_id][0:4]


VMEM = pl.BlockSpec(memory_space=pltpu.VMEM)
SMEM = pl.BlockSpec(memory_space=pltpu.SMEM)


def run_template(flags, stiffness, normals, branch_length, neighbours):
    f32 = jnp.float32
    return pl.pallas_call(
        template_kernel,
        out_shape=(
            jax.ShapeDtypeStruct((CONTACTS, SLOT_COUNT, GRAINS), f32),
            jax.ShapeDtypeStruct((SLOT_COUNT, GRAINS), f32),
            jax.ShapeDtypeStruct((21, SLOT_COUNT), f32),
            jax.ShapeDtypeStruct((32, 128), jnp.int32),
            jax.ShapeDtypeStruct((SLOT_COUNT, 4096), jnp.bfloat16),
            jax.ShapeDtypeStruct((6, CONTACTS, GRAINS), f32),
            jax.ShapeDtypeStruct((CHUNKS,), jnp.int32),
        ),
        in_specs=[VMEM] * 5,
        out_specs=(VMEM,) * 6 + (SMEM,),
        scratch_shapes=[
            pltpu.VMEM((SLOT_COUNT * CONTACTS, 128), f32),
            pltpu.VMEM((256, 128), f32),
            pltpu.VMEM((CONTACTS, 32, GRAINS), jnp.bfloat16),
            pltpu.VMEM((CONTACTS, 32, GRAINS), jnp.bfloat16),
        ],
        cost_estimate=pl.CostEstimate(flops=40_000_000, bytes_accessed=8_000_000, transcendentals=0),
        name="template",
    )(flags, stiffness, normals, branch_length, neighbours)


def run_relax(near, disp, upper, load, tangent, rank, sel, wt, cd, lp, normals, neighbours):
    f32 = jnp.float32
    return pl.pallas_call(
        relax_kernel,
        out_shape=(
            jax.ShapeDtypeStruct((3, 4, 128), f32),
            jax.ShapeDtypeStruct((3, 4, 128), f32),
            jax.ShapeDtypeStruct((192, 128), f32),
            jax.ShapeDtypeStruct((6, SLOT_COUNT), f32),
        ),
        in_specs=[SMEM] + [VMEM] * 11,
        out_specs=(VMEM,) * 4,
        scratch_shapes=[
            pltpu.VMEM((8, 128), f32),
            pltpu.VMEM((256, 128), f32),
            pltpu.VMEM((8, 4096), jnp.bfloat16),
            pltpu.VMEM((8, 4096), jnp.bfloat16),
            pltpu.VMEM((CONTACTS, SLOT_COUNT, GRAINS), f32),
            pltpu.VMEM((2, 96, GRAINS), f32),
            pltpu.VMEM((192, 128), f32),
            pltpu.VMEM((CONTACTS, 96, 128), f32),
        ],
        cost_estimate=pl.CostEstimate(
            flops=200_000_000, bytes_accessed=8_000_000, transcendentals=0
        ),
        name="relax",
    )(near, disp, upper, load, tangent, rank, sel, wt, cd, lp, normals, neighbours)


def body(
    displacement,
    load,
    elastic_tangent,
    band_flags,
    contact_stiffness,
    normals,
    branch_length,
    neighbours,
):
    upper = shifted(displacement, ("row", "col"), -1)
    wt, cd, tangent, rank, sel, lp, near = run_template(
        band_flags.reshape(32, 128), contact_stiffness, normals, branch_length, neighbours
    )
    pre, carried, stress, band = run_relax(
        near,
        displacement.reshape(3, 4, 128),
        upper.reshape(3, 4, 128),
        load.reshape(3, 4, 128),
        elastic_tangent.reshape(672, 128),
        rank,
        sel,
        wt,
        cd,
        lp,
        normals,
        neighbours,
    )
    arrived = shifted(carried, ("row", "col"), 1)
    residual = (pre - arrived).reshape(3, 1, 4, 128)
    return (residual, stress.reshape(6, 8, 1, 4, 128), tangent, band)


def solution(mesh):
    placed = (
        P(None, ("row", "col"), None, None),
        P(None, ("row", "col"), None, None),
        P(None, None, ("row", "col"), None, None),
        P(None, ("row", "col"), None, None),
        P(("row", "col"), None, None),
        P(),
        P(),
        P(),
    )
    return jax.shard_map(
        body,
        mesh=mesh,
        in_specs=placed,
        out_specs=(
            P(None, ("row", "col"), None, None),
            P(None, None, ("row", "col"), None, None),
            P(None, ("row", "col")),
            P(None, ("row", "col")),
        ),
        check_vma=False,
    )
```

```python
import jax
import jax.numpy as jnp
import numpy as np
from jax import lax
from jax.experimental import pallas as pl
from jax.experimental.pallas import tpu as pltpu
from jax.sharding import PartitionSpec as P

SWEEPS = 4
RELAX_FACTOR = 0.8
LOW = float(0.5 - 0.5 / np.sqrt(3.0))
HIGH = float(0.5 + 0.5 / np.sqrt(3.0))
GRAINS = 2048
CONTACTS = 8
SLOT_COUNT = 32
GROUPS = SLOT_COUNT // 8
CHUNKS = GRAINS // 128
UNROLL = 4
PAIRS = [(row_id, col_id) for row_id in range(6) for col_id in range(row_id, 6)]
NT = (((1,), (1,)), ((), ()))


def shifted(value, axis, steps):
    count = lax.axis_size(axis)
    leading, last = (max(0, -steps), min(count, count - steps))
    return lax.ppermute(value, axis, [(source, source + steps) for source in range(leading, last)])


def lanes_of(chunk):
    return pl.ds(pl.multiple_of(chunk * 128, 128), 128)


def row8(ref, row, lanes):
    return jnp.broadcast_to(ref[row : row + 1, lanes], (8, 128))


LANE_GATHER = lax.GatherDimensionNumbers(
    offset_dims=(),
    collapsed_slice_dims=(1,),
    start_index_map=(1,),
    operand_batching_dims=(0,),
    start_indices_batching_dims=(0,),
)


def take_lanes(table, index):
    return lax.gather(
        table,
        index[..., None],
        LANE_GATHER,
        slice_sizes=(1, 1),
        mode=lax.GatherScatterMode.PROMISE_IN_BOUNDS,
    )


def template_kernel(
    flags_ref,
    stiff_ref,
    nrm_ref,
    br_ref,
    nbr_ref,
    wt_ref,
    cd_ref,
    tan_ref,
    rank_ref,
    sel_ref,
    lp_ref,
    raw_ref,
    basis_ref,
    high_ref,
    low_ref,
):
    flags = flags_ref[...]
    flags_f = flags.astype(jnp.float32)
    tri = (
        lax.broadcasted_iota(jnp.int32, (128, 128), 0)
        <= lax.broadcasted_iota(jnp.int32, (128, 128), 1)
    ).astype(jnp.float32)
    inside = jnp.dot(flags_f, tri, preferred_element_type=jnp.float32)
    before = (
        lax.broadcasted_iota(jnp.int32, (32, 32), 1) < lax.broadcasted_iota(jnp.int32, (32, 32), 0)
    ).astype(jnp.float32)
    ahead = jnp.sum(
        jnp.dot(before, flags_f, preferred_element_type=jnp.float32), axis=1, keepdims=True
    )
    rank = jnp.where(flags == 1, (inside + ahead - 1.0).astype(jnp.int32), -1)
    rank_ref[...] = rank
    live_total = jnp.sum(flags_f)
    slot_rows = lax.broadcasted_iota(jnp.int32, (32, 128), 0)
    for row in range(32):
        picked = jnp.broadcast_to(rank_ref[row : row + 1, :], (32, 128)) == slot_rows
        sel_ref[:, row * 128 : (row + 1) * 128] = jnp.where(picked, 1.0, 0.0).astype(jnp.bfloat16)

    basis_ref[168:256, :] = jnp.zeros((88, 128), jnp.float32)

    def chunk_step(chunk, carry):
        lanes = lanes_of(chunk)
        names = nbr_ref[:, lanes]
        own = lax.broadcasted_iota(jnp.int32, (8, 128), 1) + chunk * 128
        mask = jnp.where(names != own, 1.0, 0.0)
        n0, n1, n2 = (nrm_ref[axis_id, :, lanes] for axis_id in range(3))
        length = br_ref[:, lanes]
        proj = [n0 * n0, n1 * n1, n2 * n2, n1 * n2, n0 * n2, n0 * n1]
        scaled = [length * value for value in proj]
        for comp in range(6):
            lp_ref[comp, :, lanes] = scaled[comp]
        for place, (row_id, col_id) in enumerate(PAIRS):
            basis_ref[place * 8 : (place + 1) * 8, :] = scaled[row_id] * scaled[col_id]
        for contact in range(CONTACTS):
            basis = basis_ref[pl.ds(contact, 32, stride=8), :]
            high = basis.astype(jnp.bfloat16)
            high_ref[contact, :, lanes] = high
            low_ref[contact, :, lanes] = (basis - high.astype(jnp.float32)).astype(jnp.bfloat16)
        for slot in range(SLOT_COUNT):
            raw_ref[slot * 8 : (slot + 1) * 8, :] = (
                stiff_ref[slot, :, lanes].astype(jnp.float32) * mask
            )
        for group in range(GROUPS):
            total = None
            for contact in range(CONTACTS):
                value = raw_ref[pl.ds(group * 64 + contact, 8, stride=8), :]
                wt_ref[contact, group * 8 : (group + 1) * 8, lanes] = value
                total = value if total is None else total + value
            cd_ref[group * 8 : (group + 1) * 8, lanes] = RELAX_FACTOR / total
        return carry

    lax.fori_loop(0, CHUNKS, chunk_step, 0)

    acc = jnp.zeros((32, 32), jnp.float32)
    for contact in range(CONTACTS):
        weights = wt_ref[contact].astype(jnp.bfloat16)
        for part_ref in (high_ref, low_ref):
            acc = acc + lax.dot_general(
                part_ref[contact], weights, NT, preferred_element_type=jnp.float32
            )
    slot_lane = lax.broadcasted_iota(jnp.int32, (32, 32), 1).astype(jnp.float32)
    acc = jnp.where(slot_lane < live_total, acc * (1.0 / GRAINS), 0.0)
    tan_ref[...] = acc[:21]


def lerp(low_value, high_value, bit):
    weight = HIGH if bit else LOW
    return low_value + weight * (high_value - low_value)


def strain_rows(plane_refs, dup_ref):
    row = lax.broadcasted_iota(jnp.int32, (8, 128), 0)
    lane = lax.broadcasted_iota(jnp.int32, (8, 128), 1)
    z_weight = jnp.where(row < 4, LOW, HIGH)
    last_y = (row & 3) == 3
    last_z = lane == 127
    gradient = {}
    for axis_id in range(3):
        along, slope = {}, {}
        for bit_x in range(2):
            plane = plane_refs[bit_x][axis_id]
            dup_ref[0:4, :] = plane
            dup_ref[4:8, :] = plane
            base = dup_ref[...]
            for bit_y in range(2):
                value = base if bit_y == 0 else jnp.where(last_y, 0.0, pltpu.roll(base, 7, 0))
                after = jnp.where(last_z, 0.0, pltpu.roll(value, 127, 1))
                slope[bit_x, bit_y] = after - value
                along[bit_x, bit_y] = value + z_weight * (after - value)
        for gauss_y in range(2):
            for gauss_x in range(2):
                point = 2 * gauss_x + gauss_y
                face = [lerp(along[bit_x, 0], along[bit_x, 1], gauss_y) for bit_x in range(2)]
                gradient[point, axis_id, 0] = face[1] - face[0]
                gradient[point, axis_id, 1] = lerp(
                    along[0, 1] - along[0, 0], along[1, 1] - along[1, 0], gauss_x
                )
                edge = [lerp(slope[bit_x, 0], slope[bit_x, 1], gauss_y) for bit_x in range(2)]
                gradient[point, axis_id, 2] = lerp(edge[0], edge[1], gauss_x)
    return [
        [
            gradient[point, 0, 0],
            gradient[point, 1, 1],
            gradient[point, 2, 2],
            gradient[point, 1, 2] + gradient[point, 2, 1],
            gradient[point, 0, 2] + gradient[point, 2, 0],
            gradient[point, 0, 1] + gradient[point, 1, 0],
        ]
        for point in range(4)
    ]


def weigh(low_value, high_value, corner_bit):
    if corner_bit:
        return LOW * low_value + HIGH * high_value
    return HIGH * low_value + LOW * high_value


def force_rows(stress):
    row = lax.broadcasted_iota(jnp.int32, (8, 128), 0)
    lane = lax.broadcasted_iota(jnp.int32, (8, 128), 1)
    z_high = jnp.where(row < 4, LOW, HIGH)
    z_low = jnp.where(row < 4, HIGH, LOW)
    voigt = [[0, 5, 4], [5, 1, 3], [4, 3, 2]]
    planes = [[None] * 3, [None] * 3]
    for axis_id in range(3):
        part = [[stress[point][voigt[axis_id][other]] for point in range(4)] for other in range(3)]
        flow = [part[0][gauss_y] + part[0][2 + gauss_y] for gauss_y in range(2)]
        for bit_x in range(2):
            side_y = [weigh(part[1][gauss_y], part[1][2 + gauss_y], bit_x) for gauss_y in range(2)]
            side_z = [weigh(part[2][gauss_y], part[2][2 + gauss_y], bit_x) for gauss_y in range(2)]
            total_y = side_y[0] + side_y[1]
            total = None
            for bit_y in range(2):
                first = weigh(flow[0], flow[1], bit_y)
                first = first if bit_x else -first
                first = first + total_y if bit_y else first - total_y
                second = weigh(side_z[0], side_z[1], bit_y)
                near = z_low * first - second
                far = z_high * first + second
                far = jnp.where(lane == 0, 0.0, pltpu.roll(far, 1, 1))
                both = near + far
                both = both + pltpu.roll(both, 4, 0)
                if bit_y:
                    both = jnp.where((row & 3) == 0, 0.0, pltpu.roll(both, 1, 0))
                total = both if total is None else total + both
            planes[bit_x][axis_id] = 0.125 * total
    return planes


def relax_kernel(
    disp_ref,
    upper_ref,
    load_ref,
    tangent_ref,
    rank_ref,
    sel_ref,
    wt_ref,
    cd_ref,
    lp_ref,
    nrm_ref,
    nbr_ref,
    tan_ref,
    pre_ref,
    carried_ref,
    stress_ref,
    band_ref,
    dup_ref,
    strain_ref,
    split_high_ref,
    split_low_ref,
    first_ref,
    fluct_a_ref,
    fluct_b_ref,
    sums_ref,
    onehot_ref,
    moved_ref,
    names_ref,
    near_ref,
):
    near_total = 0
    for chunk in range(CHUNKS):
        reach = (nbr_ref[:, chunk * 128 : (chunk + 1) * 128] - (chunk * 128 - 64)) & (GRAINS - 1)
        near_one = (jnp.max(reach.astype(jnp.float32)) < 256.0).astype(jnp.int32)
        near_ref[chunk] = near_one
        near_total = near_total + near_one
    all_near = near_total == CHUNKS

    tiles = strain_rows((disp_ref, upper_ref), dup_ref)
    for point in range(4):
        for comp in range(6):
            start = comp * 32 + point * 8
            strain_ref[start : start + 8, :] = tiles[point][comp]
    strain_ref[192:256, :] = jnp.zeros((64, 128), jnp.float32)

    for row in range(32):
        value = strain_ref[pl.ds(row, 8, stride=32), :]
        high = value.astype(jnp.bfloat16)
        split_high_ref[:, row * 128 : (row + 1) * 128] = high
        split_low_ref[:, row * 128 : (row + 1) * 128] = (value - high.astype(jnp.float32)).astype(
            jnp.bfloat16
        )
    sel = sel_ref[...]
    slot_strain = lax.dot_general(
        sel, split_high_ref[...], NT, preferred_element_type=jnp.float32
    ) + lax.dot_general(sel, split_low_ref[...], NT, preferred_element_type=jnp.float32)
    columns = [
        [
            jnp.broadcast_to(slot_strain[group * 8 : (group + 1) * 8, comp : comp + 1], (8, 128))
            for comp in range(6)
        ]
        for group in range(GROUPS)
    ]
    strain_t = lax.dot_general(
        split_high_ref[...], sel, NT, preferred_element_type=jnp.float32
    ) + lax.dot_general(split_low_ref[...], sel, NT, preferred_element_type=jnp.float32)
    sums_ref[...] = jnp.zeros((192, 128), jnp.float32)

    def first_step(chunk, carry):
        lanes = lanes_of(chunk)
        block = lax.broadcasted_iota(jnp.int32, (16, 128), 0).astype(jnp.float32)
        for contact in range(CONTACTS):
            names = jnp.broadcast_to(nbr_ref[contact : contact + 1, lanes], (16, 128))
            wanted = (names & 127) + jnp.where((names >> 7) == chunk, 0, 128)
            wanted = (wanted.astype(jnp.float32) - block).astype(jnp.bfloat16)
            onehot_ref[chunk * CONTACTS + contact] = jnp.concatenate(
                [
                    jnp.where(wanted == jnp.bfloat16(part * 16), jnp.bfloat16(1), jnp.bfloat16(0))
                    for part in range(16)
                ],
                axis=0,
            )
        for pair in range(0, GROUPS, 2):
            groups = (pair, pair + 1)
            totals = {}
            for contact in range(CONTACTS):
                basis = [row8(lp_ref.at[comp], contact, lanes) for comp in range(6)]
                normal = [row8(nrm_ref.at[axis_id], contact, lanes) for axis_id in range(3)]
                for group in groups:
                    rows = slice(group * 8, (group + 1) * 8)
                    affine = columns[group][0] * basis[0]
                    for comp in range(1, 6):
                        affine = affine + columns[group][comp] * basis[comp]
                    force = wt_ref[contact, rows, lanes] * affine
                    for axis_id in range(3):
                        term = force * normal[axis_id]
                        key = (group, axis_id)
                        totals[key] = totals[key] + term if contact else term
            for group in groups:
                factor = cd_ref[group * 8 : (group + 1) * 8, lanes]
                for axis_id in range(3):
                    start = axis_id * 32 + group * 8
                    first_ref[start : start + 8, lanes] = factor * totals[group, axis_id]
        return carry

    lax.fori_loop(0, CHUNKS, first_step, 0)

    half = lax.broadcasted_iota(jnp.int32, (8, 128), 1) < 64

    def gather_near(source_ref, chunk, moved_ref):
        lanes = lanes_of(chunk)
        lanes_up = lanes_of((chunk + 1) & (CHUNKS - 1))
        lanes_down = lanes_of((chunk + CHUNKS - 1) & (CHUNKS - 1))
        tiles = [slice(tile * 8, (tile + 1) * 8) for tile in range(12)]
        own = [source_ref[tile, lanes] for tile in tiles]
        sides = [
            jnp.where(half, source_ref[tile, lanes_up], source_ref[tile, lanes_down])
            for tile in tiles
        ]
        for contact in range(CONTACTS):
            names = row8(nbr_ref, contact, lanes)
            index = names & 127
            inside = (names >> 7) == chunk
            for place, tile in enumerate(tiles):
                moved_ref[tile, contact * 128 : (contact + 1) * 128] = jnp.where(
                    inside, take_lanes(own[place], index), take_lanes(sides[place], index)
                )

    tall = lax.broadcasted_iota(jnp.int32, (96, 128), 1) < 64

    def dot_pieces(source_ref, chunk):
        lanes = lanes_of(chunk)
        lanes_up = lanes_of((chunk + 1) & (CHUNKS - 1))
        lanes_down = lanes_of((chunk + CHUNKS - 1) & (CHUNKS - 1))
        own = source_ref[:, lanes]
        sides = jnp.where(tall, source_ref[:, lanes_up], source_ref[:, lanes_down])
        window = jnp.concatenate([own, sides], axis=1)
        high = window.astype(jnp.bfloat16)
        low = (window - high.astype(jnp.float32)).astype(jnp.bfloat16)
        both = jnp.concatenate([high, low], axis=0)

        def pieces(pair):
            place = chunk * CONTACTS + 2 * pair
            picks = jnp.concatenate([onehot_ref[place], onehot_ref[place + 1]], axis=1)
            value = jnp.dot(both, picks, preferred_element_type=jnp.float32)
            return value[0:96] + value[96:192]

        return pieces

    def scratch_pieces(moved_ref):
        return lambda pair: moved_ref[:, pair * 256 : (pair + 1) * 256]

    def chunk_forces(source_ref, chunk, pieces, use):
        lanes = lanes_of(chunk)
        own = [source_ref[tile * 8 : (tile + 1) * 8, lanes] for tile in range(12)]
        for pair in range(CONTACTS // 2):
            moved = pieces(pair)
            for half_id in range(2):
                contact = 2 * pair + half_id
                columns_of = slice(half_id * 128, (half_id + 1) * 128)
                normal = [row8(nrm_ref.at[axis_id], contact, lanes) for axis_id in range(3)]
                for group in range(GROUPS):
                    stretch = None
                    for axis_id in range(3):
                        tile = axis_id * 4 + group
                        there = moved[tile * 8 : (tile + 1) * 8, columns_of]
                        term = normal[axis_id] * (there - own[tile])
                        stretch = term if stretch is None else stretch + term
                    rows = slice(group * 8, (group + 1) * 8)
                    use(contact, group, wt_ref[contact, rows, lanes] * stretch, normal)
        return own

    def gather_far(source_ref, chunk, moved_ref):
        lanes = lanes_of(chunk)
        for contact in range(CONTACTS):
            names_ref[contact] = row8(nbr_ref, contact, lanes)

        def contact_step(contact, carry):
            names = names_ref[contact]
            index = names & 127
            block = names >> 7

            def step(place, values):
                hit = block == place
                return tuple(
                    jnp.where(
                        hit,
                        take_lanes(source_ref[tile * 8 : (tile + 1) * 8, lanes_of(place)], index),
                        values[tile],
                    )
                    for tile in range(12)
                )

            zero = jnp.zeros((8, 128), jnp.float32)
            values = lax.fori_loop(0, CHUNKS, step, (zero,) * 12)
            for tile in range(12):
                moved_ref[tile * 8 : (tile + 1) * 8, lanes_of(contact)] = values[tile]
            return carry

        lax.fori_loop(0, CONTACTS, contact_step, 0)

    def all_chunks(source_ref, work):
        @pl.when(all_near)
        def _():
            def step(turn, carry):
                for place in range(UNROLL):
                    chunk = turn * UNROLL + place
                    work(chunk, dot_pieces(source_ref, chunk))
                return carry

            lax.fori_loop(0, CHUNKS // UNROLL, step, 0)

        @pl.when(jnp.logical_not(all_near))
        def _():
            def step(chunk, carry):
                near = near_ref[chunk] == 1

                @pl.when(near)
                def _():
                    gather_near(source_ref, chunk, moved_ref)

                @pl.when(jnp.logical_not(near))
                def _():
                    gather_far(source_ref, chunk, moved_ref)

                work(chunk, scratch_pieces(moved_ref))
                return carry

            lax.fori_loop(0, CHUNKS, step, 0)

    def sweep(source_ref, target_ref):
        def work(chunk, pieces):
            totals = [None] * 12

            def use(contact, group, force, normal):
                for axis_id in range(3):
                    tile = axis_id * 4 + group
                    term = force * normal[axis_id]
                    totals[tile] = totals[tile] + term if contact else term

            own = chunk_forces(source_ref, chunk, pieces, use)
            lanes = lanes_of(chunk)
            for group in range(GROUPS):
                factor = cd_ref[group * 8 : (group + 1) * 8, lanes]
                for axis_id in range(3):
                    tile = axis_id * 4 + group
                    rows = slice(tile * 8, (tile + 1) * 8)
                    target_ref[rows, lanes] = own[tile] + first_ref[rows, lanes] + factor * totals[tile]

        all_chunks(source_ref, work)

    def stress_work(chunk, pieces):
        lanes = lanes_of(chunk)
        totals = [None] * 24

        def use(contact, group, force, normal):
            for comp in range(6):
                tile = comp * 4 + group
                term = force * row8(lp_ref.at[comp], contact, lanes)
                totals[tile] = totals[tile] + term if contact else term

        chunk_forces(current, chunk, pieces, use)
        for tile in range(24):
            sums_ref[tile * 8 : (tile + 1) * 8, :] += totals[tile]

    current = first_ref
    for turn in range(SWEEPS - 1):
        target = fluct_b_ref if turn % 2 else fluct_a_ref
        sweep(current, target)
        current = target
    all_chunks(current, stress_work)

    lane32 = lax.broadcasted_iota(jnp.int32, (32, 128), 1)
    table = jnp.zeros((32, 128), jnp.float32)
    for comp in range(6):
        total = jnp.sum(sums_ref[comp * 32 : (comp + 1) * 32, :], axis=1, keepdims=True)
        table = jnp.where(lane32 == comp, total * (1.0 / GRAINS), table)
    full = jnp.concatenate([table, jnp.zeros((96, 128), jnp.float32)], axis=0)
    shares = []
    for row_id in range(6):
        share = None
        for col_id in range(6):
            where = PAIRS.index((min(row_id, col_id), max(row_id, col_id)))
            term = tan_ref[where : where + 1, :] * strain_t[col_id : col_id + 1, :]
            share = term if share is None else share + term
        shares.append(share)
    flipped = jnp.transpose(full)[0:6, 0:32] + jnp.concatenate(shares, axis=0)
    band_ref[...] = flipped
    dup_ref[0:6, 0:32] = flipped

    strain = [strain_ref[comp * 32 : (comp + 1) * 32, :] for comp in range(6)]
    rank = rank_ref[...]
    banded = rank >= 0
    place = jnp.maximum(rank, 0)
    stress = []
    for row_id in range(6):
        running = None
        for col_id in range(6):
            where = PAIRS.index((min(row_id, col_id), max(row_id, col_id)))
            term = (
                tangent_ref[where * 32 : (where + 1) * 32, :].astype(jnp.float32) * strain[col_id]
            )
            running = term if running is None else running + term
        values = take_lanes(jnp.broadcast_to(dup_ref[row_id : row_id + 1, :], (32, 128)), place)
        value = jnp.where(banded, values, running)
        stress_ref[row_id * 32 : (row_id + 1) * 32, :] = value
        stress.append(value)
    planes = force_rows(
        [[stress[comp][point * 8 : (point + 1) * 8, :] for comp in range(6)] for point in range(4)]
    )
    for axis_id in range(3):
        pre_ref[axis_id] = load_ref[axis_id] - planes[0][axis_id][0:4]
        carried_ref[axis_id] = planes[1][axis_id][0:4]


VMEM = pl.BlockSpec(memory_space=pltpu.VMEM)


def run_template(flags, stiffness, normals, branch_length, neighbours):
    f32 = jnp.float32
    return pl.pallas_call(
        template_kernel,
        out_shape=(
            jax.ShapeDtypeStruct((CONTACTS, SLOT_COUNT, GRAINS), f32),
            jax.ShapeDtypeStruct((SLOT_COUNT, GRAINS), f32),
            jax.ShapeDtypeStruct((21, SLOT_COUNT), f32),
            jax.ShapeDtypeStruct((32, 128), jnp.int32),
            jax.ShapeDtypeStruct((SLOT_COUNT, 4096), jnp.bfloat16),
            jax.ShapeDtypeStruct((6, CONTACTS, GRAINS), f32),
        ),
        in_specs=[VMEM] * 5,
        out_specs=(VMEM,) * 6,
        scratch_shapes=[
            pltpu.VMEM((SLOT_COUNT * CONTACTS, 128), f32),
            pltpu.VMEM((256, 128), f32),
            pltpu.VMEM((CONTACTS, 32, GRAINS), jnp.bfloat16),
            pltpu.VMEM((CONTACTS, 32, GRAINS), jnp.bfloat16),
        ],
        cost_estimate=pl.CostEstimate(flops=40_000_000, bytes_accessed=8_000_000, transcendentals=0),
        name="template",
    )(flags, stiffness, normals, branch_length, neighbours)


def run_relax(disp, upper, load, tangent, rank, sel, wt, cd, lp, normals, neighbours, tan):
    f32 = jnp.float32
    return pl.pallas_call(
        relax_kernel,
        out_shape=(
            jax.ShapeDtypeStruct((3, 4, 128), f32),
            jax.ShapeDtypeStruct((3, 4, 128), f32),
            jax.ShapeDtypeStruct((192, 128), f32),
            jax.ShapeDtypeStruct((6, SLOT_COUNT), f32),
        ),
        in_specs=[VMEM] * 12,
        out_specs=(VMEM,) * 4,
        scratch_shapes=[
            pltpu.VMEM((8, 128), f32),
            pltpu.VMEM((256, 128), f32),
            pltpu.VMEM((8, 4096), jnp.bfloat16),
            pltpu.VMEM((8, 4096), jnp.bfloat16),
            pltpu.VMEM((96, GRAINS), f32),
            pltpu.VMEM((96, GRAINS), f32),
            pltpu.VMEM((96, GRAINS), f32),
            pltpu.VMEM((192, 128), f32),
            pltpu.VMEM((CHUNKS * CONTACTS, 256, 128), jnp.bfloat16),
            pltpu.VMEM((96, CONTACTS * 128), f32),
            pltpu.VMEM((CONTACTS, 8, 128), jnp.int32),
            pltpu.SMEM((CHUNKS,), jnp.int32),
        ],
        cost_estimate=pl.CostEstimate(
            flops=200_000_000, bytes_accessed=8_000_000, transcendentals=0
        ),
        name="relax",
    )(disp, upper, load, tangent, rank, sel, wt, cd, lp, normals, neighbours, tan)


def body(
    displacement,
    load,
    elastic_tangent,
    band_flags,
    contact_stiffness,
    normals,
    branch_length,
    neighbours,
):
    upper = shifted(displacement, ("row", "col"), -1)
    wt, cd, tangent, rank, sel, lp = run_template(
        band_flags.reshape(32, 128), contact_stiffness, normals, branch_length, neighbours
    )
    pre, carried, stress, band = run_relax(
        displacement.reshape(3, 4, 128),
        upper.reshape(3, 4, 128),
        load.reshape(3, 4, 128),
        elastic_tangent.reshape(672, 128),
        rank,
        sel,
        wt,
        cd,
        lp,
        normals,
        neighbours,
        tangent,
    )
    arrived = shifted(carried, ("row", "col"), 1)
    residual = (pre - arrived).reshape(3, 1, 4, 128)
    return (residual, stress.reshape(6, 8, 1, 4, 128), tangent, band)


def solution(mesh):
    placed = (
        P(None, ("row", "col"), None, None),
        P(None, ("row", "col"), None, None),
        P(None, None, ("row", "col"), None, None),
        P(None, ("row", "col"), None, None),
        P(("row", "col"), None, None),
        P(),
        P(),
        P(),
    )
    return jax.shard_map(
        body,
        mesh=mesh,
        in_specs=placed,
        out_specs=(
            P(None, ("row", "col"), None, None),
            P(None, None, ("row", "col"), None, None),
            P(None, ("row", "col")),
            P(None, ("row", "col")),
        ),
        check_vma=False,
    )
```

```python
import jax
import jax.numpy as jnp
import numpy as np
from jax import lax
from jax.experimental import pallas as pl
from jax.experimental.pallas import tpu as pltpu
from jax.sharding import PartitionSpec as P

SWEEPS = 4
RELAX_FACTOR = 0.8
LOW = float(0.5 - 0.5 / np.sqrt(3.0))
HIGH = float(0.5 + 0.5 / np.sqrt(3.0))
GRAINS = 2048
CONTACTS = 8
SLOT_COUNT = 32
GROUPS = SLOT_COUNT // 8
CHUNKS = GRAINS // 128
UNROLL = 4
PAIRS = [(row_id, col_id) for row_id in range(6) for col_id in range(row_id, 6)]
NT = (((1,), (1,)), ((), ()))


def shifted(value, axis, steps):
    count = lax.axis_size(axis)
    leading, last = (max(0, -steps), min(count, count - steps))
    return lax.ppermute(value, axis, [(source, source + steps) for source in range(leading, last)])


def lanes_of(chunk):
    return pl.ds(pl.multiple_of(chunk * 128, 128), 128)


def row8(ref, row, lanes):
    return jnp.broadcast_to(ref[row : row + 1, lanes], (8, 128))


LANE_GATHER = lax.GatherDimensionNumbers(
    offset_dims=(),
    collapsed_slice_dims=(1,),
    start_index_map=(1,),
    operand_batching_dims=(0,),
    start_indices_batching_dims=(0,),
)


def take_lanes(table, index):
    return lax.gather(
        table,
        index[..., None],
        LANE_GATHER,
        slice_sizes=(1, 1),
        mode=lax.GatherScatterMode.PROMISE_IN_BOUNDS,
    )


def template_kernel(
    flags_hbm,
    stiff_hbm,
    nrm_hbm,
    br_hbm,
    nbr_hbm,
    disp_hbm,
    load_hbm,
    tangent_hbm,
    wt_ref,
    cd_ref,
    tan_ref,
    tan_copy_ref,
    rank_ref,
    sel_ref,
    lp_ref,
    nrm_ref,
    nbr_ref,
    disp_ref,
    load_ref,
    tangent_ref,
    raw_ref,
    basis_ref,
    high_ref,
    low_ref,
    flags_ref,
    stiff_ref,
    br_ref,
    small_sems,
    stiff_sems,
):
    small = [
        pltpu.make_async_copy(source, target, small_sems.at[place])
        for place, (source, target) in enumerate(
            [
                (flags_hbm, flags_ref),
                (nrm_hbm, nrm_ref),
                (br_hbm, br_ref),
                (nbr_hbm, nbr_ref),
                (disp_hbm, disp_ref),
                (load_hbm, load_ref),
                (tangent_hbm, tangent_ref),
            ]
        )
    ]
    quarter = GRAINS // 4
    big = [
        pltpu.make_async_copy(
            stiff_hbm.at[:, :, pl.ds(part * quarter, quarter)],
            stiff_ref.at[:, :, pl.ds(part * quarter, quarter)],
            stiff_sems.at[part],
        )
        for part in range(4)
    ]
    for copy in small[:4] + big + small[4:]:
        copy.start()
    for copy in small[:4]:
        copy.wait()

    flags = flags_ref[...]
    flags_f = flags.astype(jnp.float32)
    tri = (
        lax.broadcasted_iota(jnp.int32, (128, 128), 0)
        <= lax.broadcasted_iota(jnp.int32, (128, 128), 1)
    ).astype(jnp.float32)
    inside = jnp.dot(flags_f, tri, preferred_element_type=jnp.float32)
    before = (
        lax.broadcasted_iota(jnp.int32, (32, 32), 1) < lax.broadcasted_iota(jnp.int32, (32, 32), 0)
    ).astype(jnp.float32)
    ahead = jnp.sum(
        jnp.dot(before, flags_f, preferred_element_type=jnp.float32), axis=1, keepdims=True
    )
    rank = jnp.where(flags == 1, (inside + ahead - 1.0).astype(jnp.int32), -1)
    rank_ref[...] = rank
    live_total = jnp.sum(flags_f)
    slot_rows = lax.broadcasted_iota(jnp.int32, (32, 128), 0)
    for row in range(32):
        picked = jnp.broadcast_to(rank_ref[row : row + 1, :], (32, 128)) == slot_rows
        sel_ref[:, row * 128 : (row + 1) * 128] = jnp.where(picked, 1.0, 0.0).astype(jnp.bfloat16)

    basis_ref[168:256, :] = jnp.zeros((88, 128), jnp.float32)

    def chunk_step(chunk, carry):
        lanes = lanes_of(chunk)
        names = nbr_ref[:, lanes]
        own = lax.broadcasted_iota(jnp.int32, (8, 128), 1) + chunk * 128
        mask = jnp.where(names != own, 1.0, 0.0)
        n0, n1, n2 = (nrm_ref[axis_id, :, lanes] for axis_id in range(3))
        length = br_ref[:, lanes]
        proj = [n0 * n0, n1 * n1, n2 * n2, n1 * n2, n0 * n2, n0 * n1]
        scaled = [length * value for value in proj]
        for comp in range(6):
            lp_ref[comp, :, lanes] = scaled[comp]
        for place, (row_id, col_id) in enumerate(PAIRS):
            basis_ref[place * 8 : (place + 1) * 8, :] = scaled[row_id] * scaled[col_id]
        for contact in range(CONTACTS):
            basis = basis_ref[pl.ds(contact, 32, stride=8), :]
            high = basis.astype(jnp.bfloat16)
            high_ref[contact, :, lanes] = high
            low_ref[contact, :, lanes] = (basis - high.astype(jnp.float32)).astype(jnp.bfloat16)
        for slot in range(SLOT_COUNT):
            raw_ref[slot * 8 : (slot + 1) * 8, :] = (
                stiff_ref[slot, :, lanes].astype(jnp.float32) * mask
            )
        for group in range(GROUPS):
            total = None
            for contact in range(CONTACTS):
                value = raw_ref[pl.ds(group * 64 + contact, 8, stride=8), :]
                wt_ref[contact, group * 8 : (group + 1) * 8, lanes] = value
                total = value if total is None else total + value
            cd_ref[group * 8 : (group + 1) * 8, lanes] = RELAX_FACTOR / total
        return carry

    for part in range(4):
        big[part].wait()
        lax.fori_loop(part * CHUNKS // 4, (part + 1) * CHUNKS // 4, chunk_step, 0)

    acc = jnp.zeros((32, 32), jnp.float32)
    for contact in range(CONTACTS):
        weights = wt_ref[contact].astype(jnp.bfloat16)
        for part_ref in (high_ref, low_ref):
            acc = acc + lax.dot_general(
                part_ref[contact], weights, NT, preferred_element_type=jnp.float32
            )
    slot_lane = lax.broadcasted_iota(jnp.int32, (32, 32), 1).astype(jnp.float32)
    acc = jnp.where(slot_lane < live_total, acc * (1.0 / GRAINS), 0.0)
    tan_ref[...] = acc[:21]
    tan_copy_ref[...] = acc[:21]
    for copy in small[4:]:
        copy.wait()


def lerp(low_value, high_value, bit):
    weight = HIGH if bit else LOW
    return low_value + weight * (high_value - low_value)


def strain_rows(plane_refs, dup_ref):
    row = lax.broadcasted_iota(jnp.int32, (8, 128), 0)
    lane = lax.broadcasted_iota(jnp.int32, (8, 128), 1)
    z_weight = jnp.where(row < 4, LOW, HIGH)
    last_y = (row & 3) == 3
    last_z = lane == 127
    gradient = {}
    for axis_id in range(3):
        along, slope = {}, {}
        for bit_x in range(2):
            plane = plane_refs[bit_x][axis_id]
            dup_ref[0:4, :] = plane
            dup_ref[4:8, :] = plane
            base = dup_ref[...]
            for bit_y in range(2):
                value = base if bit_y == 0 else jnp.where(last_y, 0.0, pltpu.roll(base, 7, 0))
                after = jnp.where(last_z, 0.0, pltpu.roll(value, 127, 1))
                slope[bit_x, bit_y] = after - value
                along[bit_x, bit_y] = value + z_weight * (after - value)
        for gauss_y in range(2):
            for gauss_x in range(2):
                point = 2 * gauss_x + gauss_y
                face = [lerp(along[bit_x, 0], along[bit_x, 1], gauss_y) for bit_x in range(2)]
                gradient[point, axis_id, 0] = face[1] - face[0]
                gradient[point, axis_id, 1] = lerp(
                    along[0, 1] - along[0, 0], along[1, 1] - along[1, 0], gauss_x
                )
                edge = [lerp(slope[bit_x, 0], slope[bit_x, 1], gauss_y) for bit_x in range(2)]
                gradient[point, axis_id, 2] = lerp(edge[0], edge[1], gauss_x)
    return [
        [
            gradient[point, 0, 0],
            gradient[point, 1, 1],
            gradient[point, 2, 2],
            gradient[point, 1, 2] + gradient[point, 2, 1],
            gradient[point, 0, 2] + gradient[point, 2, 0],
            gradient[point, 0, 1] + gradient[point, 1, 0],
        ]
        for point in range(4)
    ]


def weigh(low_value, high_value, corner_bit):
    if corner_bit:
        return LOW * low_value + HIGH * high_value
    return HIGH * low_value + LOW * high_value


def force_rows(stress):
    row = lax.broadcasted_iota(jnp.int32, (8, 128), 0)
    lane = lax.broadcasted_iota(jnp.int32, (8, 128), 1)
    z_high = jnp.where(row < 4, LOW, HIGH)
    z_low = jnp.where(row < 4, HIGH, LOW)
    voigt = [[0, 5, 4], [5, 1, 3], [4, 3, 2]]
    planes = [[None] * 3, [None] * 3]
    for axis_id in range(3):
        part = [[stress[point][voigt[axis_id][other]] for point in range(4)] for other in range(3)]
        flow = [part[0][gauss_y] + part[0][2 + gauss_y] for gauss_y in range(2)]
        for bit_x in range(2):
            side_y = [weigh(part[1][gauss_y], part[1][2 + gauss_y], bit_x) for gauss_y in range(2)]
            side_z = [weigh(part[2][gauss_y], part[2][2 + gauss_y], bit_x) for gauss_y in range(2)]
            total_y = side_y[0] + side_y[1]
            total = None
            for bit_y in range(2):
                first = weigh(flow[0], flow[1], bit_y)
                first = first if bit_x else -first
                first = first + total_y if bit_y else first - total_y
                second = weigh(side_z[0], side_z[1], bit_y)
                near = z_low * first - second
                far = z_high * first + second
                far = jnp.where(lane == 0, 0.0, pltpu.roll(far, 1, 1))
                both = near + far
                both = both + pltpu.roll(both, 4, 0)
                if bit_y:
                    both = jnp.where((row & 3) == 0, 0.0, pltpu.roll(both, 1, 0))
                total = both if total is None else total + both
            planes[bit_x][axis_id] = 0.125 * total
    return planes


def relax_kernel(
    disp_ref,
    upper_ref,
    load_ref,
    tangent_ref,
    rank_ref,
    sel_ref,
    wt_ref,
    cd_ref,
    lp_ref,
    nrm_ref,
    nbr_ref,
    tan_ref,
    pre_ref,
    carried_ref,
    stress_ref,
    band_ref,
    dup_ref,
    strain_ref,
    split_high_ref,
    split_low_ref,
    first_ref,
    fluct_a_ref,
    fluct_b_ref,
    sums_ref,
    onehot_ref,
    moved_ref,
    names_ref,
    near_ref,
):
    near_total = 0
    for chunk in range(CHUNKS):
        reach = (nbr_ref[:, chunk * 128 : (chunk + 1) * 128] - (chunk * 128 - 64)) & (GRAINS - 1)
        near_one = (jnp.max(reach.astype(jnp.float32)) < 256.0).astype(jnp.int32)
        near_ref[chunk] = near_one
        near_total = near_total + near_one
    all_near = near_total == CHUNKS

    tiles = strain_rows((disp_ref, upper_ref), dup_ref)
    for point in range(4):
        for comp in range(6):
            start = comp * 32 + point * 8
            strain_ref[start : start + 8, :] = tiles[point][comp]
    strain_ref[192:256, :] = jnp.zeros((64, 128), jnp.float32)

    for row in range(32):
        value = strain_ref[pl.ds(row, 8, stride=32), :]
        high = value.astype(jnp.bfloat16)
        split_high_ref[:, row * 128 : (row + 1) * 128] = high
        split_low_ref[:, row * 128 : (row + 1) * 128] = (value - high.astype(jnp.float32)).astype(
            jnp.bfloat16
        )
    sel = sel_ref[...]
    slot_strain = lax.dot_general(
        sel, split_high_ref[...], NT, preferred_element_type=jnp.float32
    ) + lax.dot_general(sel, split_low_ref[...], NT, preferred_element_type=jnp.float32)
    columns = [
        [
            jnp.broadcast_to(slot_strain[group * 8 : (group + 1) * 8, comp : comp + 1], (8, 128))
            for comp in range(6)
        ]
        for group in range(GROUPS)
    ]
    strain_t = lax.dot_general(
        split_high_ref[...], sel, NT, preferred_element_type=jnp.float32
    ) + lax.dot_general(split_low_ref[...], sel, NT, preferred_element_type=jnp.float32)
    sums_ref[...] = jnp.zeros((192, 128), jnp.float32)

    def first_step(chunk, carry):
        lanes = lanes_of(chunk)
        block = lax.broadcasted_iota(jnp.int32, (16, 128), 0).astype(jnp.float32)
        for contact in range(CONTACTS):
            names = jnp.broadcast_to(nbr_ref[contact : contact + 1, lanes], (16, 128))
            wanted = (names & 127) + jnp.where((names >> 7) == chunk, 0, 128)
            wanted = (wanted.astype(jnp.float32) - block).astype(jnp.bfloat16)
            onehot_ref[chunk * CONTACTS + contact] = jnp.concatenate(
                [
                    jnp.where(wanted == jnp.bfloat16(part * 16), jnp.bfloat16(1), jnp.bfloat16(0))
                    for part in range(16)
                ],
                axis=0,
            )
        for pair in range(0, GROUPS, 2):
            groups = (pair, pair + 1)
            totals = {}
            for contact in range(CONTACTS):
                basis = [row8(lp_ref.at[comp], contact, lanes) for comp in range(6)]
                normal = [row8(nrm_ref.at[axis_id], contact, lanes) for axis_id in range(3)]
                for group in groups:
                    rows = slice(group * 8, (group + 1) * 8)
                    affine = columns[group][0] * basis[0]
                    for comp in range(1, 6):
                        affine = affine + columns[group][comp] * basis[comp]
                    force = wt_ref[contact, rows, lanes] * affine
                    for axis_id in range(3):
                        term = force * normal[axis_id]
                        key = (group, axis_id)
                        totals[key] = totals[key] + term if contact else term
            for group in groups:
                factor = cd_ref[group * 8 : (group + 1) * 8, lanes]
                for axis_id in range(3):
                    start = axis_id * 32 + group * 8
                    first_ref[start : start + 8, lanes] = factor * totals[group, axis_id]
        return carry

    lax.fori_loop(0, CHUNKS, first_step, 0)

    half = lax.broadcasted_iota(jnp.int32, (8, 128), 1) < 64

    def gather_near(source_ref, chunk, moved_ref):
        lanes = lanes_of(chunk)
        lanes_up = lanes_of((chunk + 1) & (CHUNKS - 1))
        lanes_down = lanes_of((chunk + CHUNKS - 1) & (CHUNKS - 1))
        tiles = [slice(tile * 8, (tile + 1) * 8) for tile in range(12)]
        own = [source_ref[tile, lanes] for tile in tiles]
        sides = [
            jnp.where(half, source_ref[tile, lanes_up], source_ref[tile, lanes_down])
            for tile in tiles
        ]
        for contact in range(CONTACTS):
            names = row8(nbr_ref, contact, lanes)
            index = names & 127
            inside = (names >> 7) == chunk
            for place, tile in enumerate(tiles):
                moved_ref[tile, contact * 128 : (contact + 1) * 128] = jnp.where(
                    inside, take_lanes(own[place], index), take_lanes(sides[place], index)
                )

    tall = lax.broadcasted_iota(jnp.int32, (96, 128), 1) < 64

    def dot_pieces(source_ref, chunk):
        lanes = lanes_of(chunk)
        lanes_up = lanes_of((chunk + 1) & (CHUNKS - 1))
        lanes_down = lanes_of((chunk + CHUNKS - 1) & (CHUNKS - 1))
        own = source_ref[:, lanes]
        sides = jnp.where(tall, source_ref[:, lanes_up], source_ref[:, lanes_down])
        window = jnp.concatenate([own, sides], axis=1)
        high = window.astype(jnp.bfloat16)
        low = (window - high.astype(jnp.float32)).astype(jnp.bfloat16)
        both = jnp.concatenate([high, low], axis=0)

        def pieces(pair):
            place = chunk * CONTACTS + 2 * pair
            picks = jnp.concatenate([onehot_ref[place], onehot_ref[place + 1]], axis=1)
            value = jnp.dot(both, picks, preferred_element_type=jnp.float32)
            return value[0:96] + value[96:192]

        return pieces

    def scratch_pieces(moved_ref):
        return lambda pair: moved_ref[:, pair * 256 : (pair + 1) * 256]

    def chunk_forces(source_ref, chunk, pieces, use):
        lanes = lanes_of(chunk)
        own = [source_ref[tile * 8 : (tile + 1) * 8, lanes] for tile in range(12)]
        for pair in range(CONTACTS // 2):
            moved = pieces(pair)
            for half_id in range(2):
                contact = 2 * pair + half_id
                columns_of = slice(half_id * 128, (half_id + 1) * 128)
                normal = [row8(nrm_ref.at[axis_id], contact, lanes) for axis_id in range(3)]
                for group in range(GROUPS):
                    stretch = None
                    for axis_id in range(3):
                        tile = axis_id * 4 + group
                        there = moved[tile * 8 : (tile + 1) * 8, columns_of]
                        term = normal[axis_id] * (there - own[tile])
                        stretch = term if stretch is None else stretch + term
                    rows = slice(group * 8, (group + 1) * 8)
                    use(contact, group, wt_ref[contact, rows, lanes] * stretch, normal)
        return own

    def gather_far(source_ref, chunk, moved_ref):
        lanes = lanes_of(chunk)
        for contact in range(CONTACTS):
            names_ref[contact] = row8(nbr_ref, contact, lanes)

        def contact_step(contact, carry):
            names = names_ref[contact]
            index = names & 127
            block = names >> 7

            def step(place, values):
                hit = block == place
                return tuple(
                    jnp.where(
                        hit,
                        take_lanes(source_ref[tile * 8 : (tile + 1) * 8, lanes_of(place)], index),
                        values[tile],
                    )
                    for tile in range(12)
                )

            zero = jnp.zeros((8, 128), jnp.float32)
            values = lax.fori_loop(0, CHUNKS, step, (zero,) * 12)
            for tile in range(12):
                moved_ref[tile * 8 : (tile + 1) * 8, lanes_of(contact)] = values[tile]
            return carry

        lax.fori_loop(0, CONTACTS, contact_step, 0)

    def all_chunks(source_ref, work):
        @pl.when(all_near)
        def _():
            def step(turn, carry):
                for place in range(UNROLL):
                    chunk = turn * UNROLL + place
                    work(chunk, dot_pieces(source_ref, chunk))
                return carry

            lax.fori_loop(0, CHUNKS // UNROLL, step, 0)

        @pl.when(jnp.logical_not(all_near))
        def _():
            def step(chunk, carry):
                near = near_ref[chunk] == 1

                @pl.when(near)
                def _():
                    gather_near(source_ref, chunk, moved_ref)

                @pl.when(jnp.logical_not(near))
                def _():
                    gather_far(source_ref, chunk, moved_ref)

                work(chunk, scratch_pieces(moved_ref))
                return carry

            lax.fori_loop(0, CHUNKS, step, 0)

    def sweep(source_ref, target_ref):
        def work(chunk, pieces):
            totals = [None] * 12

            def use(contact, group, force, normal):
                for axis_id in range(3):
                    tile = axis_id * 4 + group
                    term = force * normal[axis_id]
                    totals[tile] = totals[tile] + term if contact else term

            own = chunk_forces(source_ref, chunk, pieces, use)
            lanes = lanes_of(chunk)
            for group in range(GROUPS):
                factor = cd_ref[group * 8 : (group + 1) * 8, lanes]
                for axis_id in range(3):
                    tile = axis_id * 4 + group
                    rows = slice(tile * 8, (tile + 1) * 8)
                    target_ref[rows, lanes] = own[tile] + first_ref[rows, lanes] + factor * totals[tile]

        all_chunks(source_ref, work)

    def stress_work(chunk, pieces):
        lanes = lanes_of(chunk)
        totals = [None] * 24

        def use(contact, group, force, normal):
            for comp in range(6):
                tile = comp * 4 + group
                term = force * row8(lp_ref.at[comp], contact, lanes)
                totals[tile] = totals[tile] + term if contact else term

        chunk_forces(current, chunk, pieces, use)
        for tile in range(24):
            sums_ref[tile * 8 : (tile + 1) * 8, :] += totals[tile]

    current = first_ref
    for turn in range(SWEEPS - 1):
        target = fluct_b_ref if turn % 2 else fluct_a_ref
        sweep(current, target)
        current = target
    all_chunks(current, stress_work)

    lane32 = lax.broadcasted_iota(jnp.int32, (32, 128), 1)
    table = jnp.zeros((32, 128), jnp.float32)
    for comp in range(6):
        total = jnp.sum(sums_ref[comp * 32 : (comp + 1) * 32, :], axis=1, keepdims=True)
        table = jnp.where(lane32 == comp, total * (1.0 / GRAINS), table)
    full = jnp.concatenate([table, jnp.zeros((96, 128), jnp.float32)], axis=0)
    shares = []
    for row_id in range(6):
        share = None
        for col_id in range(6):
            where = PAIRS.index((min(row_id, col_id), max(row_id, col_id)))
            term = tan_ref[where : where + 1, :] * strain_t[col_id : col_id + 1, :]
            share = term if share is None else share + term
        shares.append(share)
    flipped = jnp.transpose(full)[0:6, 0:32] + jnp.concatenate(shares, axis=0)
    band_ref[...] = flipped
    dup_ref[0:6, 0:32] = flipped

    strain = [strain_ref[comp * 32 : (comp + 1) * 32, :] for comp in range(6)]
    rank = rank_ref[...]
    banded = rank >= 0
    place = jnp.maximum(rank, 0)
    stress = []
    for row_id in range(6):
        running = None
        for col_id in range(6):
            where = PAIRS.index((min(row_id, col_id), max(row_id, col_id)))
            term = (
                tangent_ref[where * 32 : (where + 1) * 32, :].astype(jnp.float32) * strain[col_id]
            )
            running = term if running is None else running + term
        values = take_lanes(jnp.broadcast_to(dup_ref[row_id : row_id + 1, :], (32, 128)), place)
        value = jnp.where(banded, values, running)
        stress_ref[row_id * 32 : (row_id + 1) * 32, :] = value
        stress.append(value)
    planes = force_rows(
        [[stress[comp][point * 8 : (point + 1) * 8, :] for comp in range(6)] for point in range(4)]
    )
    for axis_id in range(3):
        pre_ref[axis_id] = load_ref[axis_id] - planes[0][axis_id][0:4]
        carried_ref[axis_id] = planes[1][axis_id][0:4]


VMEM = pl.BlockSpec(memory_space=pltpu.VMEM)
HBM = pl.BlockSpec(memory_space=pltpu.HBM)


def run_template(
    flags, stiffness, normals, branch_length, neighbours, displacement, load, elastic_tangent
):
    f32 = jnp.float32
    kept = [normals, neighbours, displacement, load, elastic_tangent]
    return pl.pallas_call(
        template_kernel,
        out_shape=(
            jax.ShapeDtypeStruct((CONTACTS, SLOT_COUNT, GRAINS), f32),
            jax.ShapeDtypeStruct((SLOT_COUNT, GRAINS), f32),
            jax.ShapeDtypeStruct((21, SLOT_COUNT), f32),
            jax.ShapeDtypeStruct((21, SLOT_COUNT), f32),
            jax.ShapeDtypeStruct((32, 128), jnp.int32),
            jax.ShapeDtypeStruct((SLOT_COUNT, 4096), jnp.bfloat16),
            jax.ShapeDtypeStruct((6, CONTACTS, GRAINS), f32),
        )
        + tuple(jax.ShapeDtypeStruct(value.shape, value.dtype) for value in kept),
        in_specs=[HBM] * 8,
        out_specs=(VMEM,) * 12,
        scratch_shapes=[
            pltpu.VMEM((SLOT_COUNT * CONTACTS, 128), f32),
            pltpu.VMEM((256, 128), f32),
            pltpu.VMEM((CONTACTS, 32, GRAINS), jnp.bfloat16),
            pltpu.VMEM((CONTACTS, 32, GRAINS), jnp.bfloat16),
            pltpu.VMEM((32, 128), jnp.int32),
            pltpu.VMEM((SLOT_COUNT, CONTACTS, GRAINS), jnp.bfloat16),
            pltpu.VMEM((CONTACTS, GRAINS), f32),
            pltpu.SemaphoreType.DMA((7,)),
            pltpu.SemaphoreType.DMA((4,)),
        ],
        cost_estimate=pl.CostEstimate(flops=40_000_000, bytes_accessed=8_000_000, transcendentals=0),
        compiler_params=pltpu.CompilerParams(vmem_limit_bytes=16 * 1024 * 1024),
        name="template",
    )(
        *[
            pltpu.with_memory_space_constraint(value, pltpu.HBM)
            for value in (flags, stiffness, *kept[:1], branch_length, *kept[1:])
        ]
    )


def run_relax(disp, upper, load, tangent, rank, sel, wt, cd, lp, normals, neighbours, tan):
    f32 = jnp.float32
    return pl.pallas_call(
        relax_kernel,
        out_shape=(
            jax.ShapeDtypeStruct((3, 4, 128), f32),
            jax.ShapeDtypeStruct((3, 4, 128), f32),
            jax.ShapeDtypeStruct((192, 128), f32),
            jax.ShapeDtypeStruct((6, SLOT_COUNT), f32),
        ),
        in_specs=[VMEM] * 12,
        out_specs=(VMEM,) * 4,
        scratch_shapes=[
            pltpu.VMEM((8, 128), f32),
            pltpu.VMEM((256, 128), f32),
            pltpu.VMEM((8, 4096), jnp.bfloat16),
            pltpu.VMEM((8, 4096), jnp.bfloat16),
            pltpu.VMEM((96, GRAINS), f32),
            pltpu.VMEM((96, GRAINS), f32),
            pltpu.VMEM((96, GRAINS), f32),
            pltpu.VMEM((192, 128), f32),
            pltpu.VMEM((CHUNKS * CONTACTS, 256, 128), jnp.bfloat16),
            pltpu.VMEM((96, CONTACTS * 128), f32),
            pltpu.VMEM((CONTACTS, 8, 128), jnp.int32),
            pltpu.SMEM((CHUNKS,), jnp.int32),
        ],
        cost_estimate=pl.CostEstimate(
            flops=200_000_000, bytes_accessed=8_000_000, transcendentals=0
        ),
        compiler_params=pltpu.CompilerParams(vmem_limit_bytes=28 * 1024 * 1024),
        name="relax",
    )(disp, upper, load, tangent, rank, sel, wt, cd, lp, normals, neighbours, tan)


def body(
    displacement,
    load,
    elastic_tangent,
    band_flags,
    contact_stiffness,
    normals,
    branch_length,
    neighbours,
):
    upper = shifted(displacement, ("row", "col"), -1)
    wt, cd, tangent, tan, rank, sel, lp, nrm, nbr, disp, load_here, elastic = run_template(
        band_flags.reshape(32, 128),
        contact_stiffness,
        normals,
        branch_length,
        neighbours,
        displacement.reshape(3, 4, 128),
        load.reshape(3, 4, 128),
        elastic_tangent.reshape(672, 128),
    )
    pre, carried, stress, band = run_relax(
        disp, upper.reshape(3, 4, 128), load_here, elastic, rank, sel, wt, cd, lp, nrm, nbr, tan
    )
    arrived = shifted(carried, ("row", "col"), 1)
    residual = (pre - arrived).reshape(3, 1, 4, 128)
    return (residual, stress.reshape(6, 8, 1, 4, 128), tangent, band)


def solution(mesh):
    placed = (
        P(None, ("row", "col"), None, None),
        P(None, ("row", "col"), None, None),
        P(None, None, ("row", "col"), None, None),
        P(None, ("row", "col"), None, None),
        P(("row", "col"), None, None),
        P(),
        P(),
        P(),
    )
    return jax.shard_map(
        body,
        mesh=mesh,
        in_specs=placed,
        out_specs=(
            P(None, ("row", "col"), None, None),
            P(None, None, ("row", "col"), None, None),
            P(None, ("row", "col")),
            P(None, ("row", "col")),
        ),
        check_vma=False,
    )
```

```python
import jax
import jax.numpy as jnp
import numpy as np
from jax import lax
from jax.experimental import pallas as pl
from jax.experimental.pallas import tpu as pltpu
from jax.sharding import PartitionSpec as P

SWEEPS = 4
RELAX_FACTOR = 0.8
LOW = float(0.5 - 0.5 / np.sqrt(3.0))
HIGH = float(0.5 + 0.5 / np.sqrt(3.0))
GRAINS = 2048
CONTACTS = 8
SLOT_COUNT = 32
GROUPS = SLOT_COUNT // 8
CHUNKS = GRAINS // 128
UNROLL = 4
EXACT = False
PAIRS = [(row_id, col_id) for row_id in range(6) for col_id in range(row_id, 6)]
NT = (((1,), (1,)), ((), ()))


def shifted(value, axis, steps):
    count = lax.axis_size(axis)
    leading, last = (max(0, -steps), min(count, count - steps))
    return lax.ppermute(value, axis, [(source, source + steps) for source in range(leading, last)])


def lanes_of(chunk):
    return pl.ds(pl.multiple_of(chunk * 128, 128), 128)


def row8(ref, row, lanes):
    return jnp.broadcast_to(ref[row : row + 1, lanes], (8, 128))


LANE_GATHER = lax.GatherDimensionNumbers(
    offset_dims=(),
    collapsed_slice_dims=(1,),
    start_index_map=(1,),
    operand_batching_dims=(0,),
    start_indices_batching_dims=(0,),
)


def take_lanes(table, index):
    return lax.gather(
        table,
        index[..., None],
        LANE_GATHER,
        slice_sizes=(1, 1),
        mode=lax.GatherScatterMode.PROMISE_IN_BOUNDS,
    )


def template_kernel(
    flags_hbm,
    stiff_hbm,
    nrm_hbm,
    br_hbm,
    nbr_hbm,
    disp_hbm,
    load_hbm,
    tangent_hbm,
    wt_ref,
    cd_ref,
    tan_ref,
    tan_copy_ref,
    rank_ref,
    sel_ref,
    lp_ref,
    nrm_ref,
    nbr_ref,
    disp_ref,
    load_ref,
    tangent_ref,
    raw_ref,
    basis_ref,
    split_ref,
    flags_ref,
    stiff_ref,
    br_ref,
    small_sems,
    stiff_sems,
):
    small = [
        pltpu.make_async_copy(source, target, small_sems.at[place])
        for place, (source, target) in enumerate(
            [
                (flags_hbm, flags_ref),
                (nrm_hbm, nrm_ref),
                (br_hbm, br_ref),
                (nbr_hbm, nbr_ref),
                (disp_hbm, disp_ref),
                (load_hbm, load_ref),
                (tangent_hbm, tangent_ref),
            ]
        )
    ]
    quarter = GRAINS // 4
    big = [
        pltpu.make_async_copy(
            stiff_hbm.at[:, :, pl.ds(part * quarter, quarter)],
            stiff_ref.at[:, :, pl.ds(part * quarter, quarter)],
            stiff_sems.at[part],
        )
        for part in range(4)
    ]
    for copy in small[:4] + big + small[4:]:
        copy.start()
    for copy in small[:4]:
        copy.wait()

    flags = flags_ref[...]
    flags_f = flags.astype(jnp.float32)
    tri = (
        lax.broadcasted_iota(jnp.int32, (128, 128), 0)
        <= lax.broadcasted_iota(jnp.int32, (128, 128), 1)
    ).astype(jnp.float32)
    inside = jnp.dot(flags_f, tri, preferred_element_type=jnp.float32)
    before = (
        lax.broadcasted_iota(jnp.int32, (32, 32), 1) < lax.broadcasted_iota(jnp.int32, (32, 32), 0)
    ).astype(jnp.float32)
    ahead = jnp.sum(
        jnp.dot(before, flags_f, preferred_element_type=jnp.float32), axis=1, keepdims=True
    )
    rank = jnp.where(flags == 1, (inside + ahead - 1.0).astype(jnp.int32), -1)
    rank_ref[...] = rank
    live_total = jnp.sum(flags_f)
    slot_rows = lax.broadcasted_iota(jnp.int32, (32, 128), 0)
    for row in range(32):
        picked = jnp.broadcast_to(rank_ref[row : row + 1, :], (32, 128)) == slot_rows
        sel_ref[:, row * 128 : (row + 1) * 128] = jnp.where(picked, 1.0, 0.0).astype(jnp.bfloat16)

    basis_ref[168:256, :] = jnp.zeros((88, 128), jnp.float32)

    def chunk_step(chunk, carry):
        lanes = lanes_of(chunk)
        names = nbr_ref[:, lanes]
        own = lax.broadcasted_iota(jnp.int32, (8, 128), 1) + chunk * 128
        mask = jnp.where(names != own, 1.0, 0.0)
        n0, n1, n2 = (nrm_ref[axis_id, :, lanes] for axis_id in range(3))
        length = br_ref[:, lanes]
        proj = [n0 * n0, n1 * n1, n2 * n2, n1 * n2, n0 * n2, n0 * n1]
        scaled = [length * value for value in proj]
        for comp in range(6):
            lp_ref[comp, :, lanes] = scaled[comp]
        for place, (row_id, col_id) in enumerate(PAIRS):
            basis_ref[place * 8 : (place + 1) * 8, :] = scaled[row_id] * scaled[col_id]
        for contact in range(CONTACTS):
            basis = basis_ref[pl.ds(contact, 32, stride=8), :]
            high = basis.astype(jnp.bfloat16)
            split_ref[contact, 0:32, lanes] = high
            split_ref[contact, 32:64, lanes] = (basis - high.astype(jnp.float32)).astype(
                jnp.bfloat16
            )
        for slot in range(SLOT_COUNT):
            raw_ref[slot * 8 : (slot + 1) * 8, :] = (
                stiff_ref[slot, :, lanes].astype(jnp.float32) * mask
            )
        for group in range(GROUPS):
            total = None
            for contact in range(CONTACTS):
                value = raw_ref[pl.ds(group * 64 + contact, 8, stride=8), :]
                wt_ref[contact, group * 8 : (group + 1) * 8, lanes] = value
                total = value if total is None else total + value
            cd_ref[group * 8 : (group + 1) * 8, lanes] = RELAX_FACTOR / total
        return carry

    for part in range(4):
        big[part].wait()
        lax.fori_loop(part * CHUNKS // 4, (part + 1) * CHUNKS // 4, chunk_step, 0)

    acc = jnp.zeros((64, 32), jnp.float32)
    for contact in range(CONTACTS):
        weights = wt_ref[contact].astype(jnp.bfloat16)
        acc = acc + lax.dot_general(
            split_ref[contact], weights, NT, preferred_element_type=jnp.float32
        )
    acc = acc[0:32] + acc[32:64]
    slot_lane = lax.broadcasted_iota(jnp.int32, (32, 32), 1).astype(jnp.float32)
    acc = jnp.where(slot_lane < live_total, acc * (1.0 / GRAINS), 0.0)
    tan_ref[...] = acc[:21]
    tan_copy_ref[...] = acc[:21]
    for copy in small[4:]:
        copy.wait()


def lerp(low_value, high_value, bit):
    weight = HIGH if bit else LOW
    return low_value + weight * (high_value - low_value)


def strain_rows(plane_refs, dup_ref):
    row = lax.broadcasted_iota(jnp.int32, (8, 128), 0)
    lane = lax.broadcasted_iota(jnp.int32, (8, 128), 1)
    z_weight = jnp.where(row < 4, LOW, HIGH)
    last_y = (row & 3) == 3
    last_z = lane == 127
    gradient = {}
    for axis_id in range(3):
        along, slope = {}, {}
        for bit_x in range(2):
            plane = plane_refs[bit_x][axis_id]
            dup_ref[0:4, :] = plane
            dup_ref[4:8, :] = plane
            base = dup_ref[...]
            for bit_y in range(2):
                value = base if bit_y == 0 else jnp.where(last_y, 0.0, pltpu.roll(base, 7, 0))
                after = jnp.where(last_z, 0.0, pltpu.roll(value, 127, 1))
                slope[bit_x, bit_y] = after - value
                along[bit_x, bit_y] = value + z_weight * (after - value)
        for gauss_y in range(2):
            for gauss_x in range(2):
                point = 2 * gauss_x + gauss_y
                face = [lerp(along[bit_x, 0], along[bit_x, 1], gauss_y) for bit_x in range(2)]
                gradient[point, axis_id, 0] = face[1] - face[0]
                gradient[point, axis_id, 1] = lerp(
                    along[0, 1] - along[0, 0], along[1, 1] - along[1, 0], gauss_x
                )
                edge = [lerp(slope[bit_x, 0], slope[bit_x, 1], gauss_y) for bit_x in range(2)]
                gradient[point, axis_id, 2] = lerp(edge[0], edge[1], gauss_x)
    return [
        [
            gradient[point, 0, 0],
            gradient[point, 1, 1],
            gradient[point, 2, 2],
            gradient[point, 1, 2] + gradient[point, 2, 1],
            gradient[point, 0, 2] + gradient[point, 2, 0],
            gradient[point, 0, 1] + gradient[point, 1, 0],
        ]
        for point in range(4)
    ]


def weigh(low_value, high_value, corner_bit):
    if corner_bit:
        return LOW * low_value + HIGH * high_value
    return HIGH * low_value + LOW * high_value


def force_rows(stress):
    row = lax.broadcasted_iota(jnp.int32, (8, 128), 0)
    lane = lax.broadcasted_iota(jnp.int32, (8, 128), 1)
    z_high = jnp.where(row < 4, LOW, HIGH)
    z_low = jnp.where(row < 4, HIGH, LOW)
    voigt = [[0, 5, 4], [5, 1, 3], [4, 3, 2]]
    planes = [[None] * 3, [None] * 3]
    for axis_id in range(3):
        part = [[stress[point][voigt[axis_id][other]] for point in range(4)] for other in range(3)]
        flow = [part[0][gauss_y] + part[0][2 + gauss_y] for gauss_y in range(2)]
        for bit_x in range(2):
            side_y = [weigh(part[1][gauss_y], part[1][2 + gauss_y], bit_x) for gauss_y in range(2)]
            side_z = [weigh(part[2][gauss_y], part[2][2 + gauss_y], bit_x) for gauss_y in range(2)]
            total_y = side_y[0] + side_y[1]
            total = None
            for bit_y in range(2):
                first = weigh(flow[0], flow[1], bit_y)
                first = first if bit_x else -first
                first = first + total_y if bit_y else first - total_y
                second = weigh(side_z[0], side_z[1], bit_y)
                near = z_low * first - second
                far = z_high * first + second
                far = jnp.where(lane == 0, 0.0, pltpu.roll(far, 1, 1))
                both = near + far
                both = both + pltpu.roll(both, 4, 0)
                if bit_y:
                    both = jnp.where((row & 3) == 0, 0.0, pltpu.roll(both, 1, 0))
                total = both if total is None else total + both
            planes[bit_x][axis_id] = 0.125 * total
    return planes


def relax_kernel(
    disp_ref,
    upper_ref,
    load_ref,
    tangent_ref,
    rank_ref,
    sel_ref,
    wt_ref,
    cd_ref,
    lp_ref,
    nrm_ref,
    nbr_ref,
    tan_ref,
    pre_ref,
    carried_ref,
    stress_ref,
    band_ref,
    dup_ref,
    strain_ref,
    split_high_ref,
    split_low_ref,
    first_ref,
    fluct_a_ref,
    fluct_b_ref,
    sums_ref,
    onehot_ref,
    moved_ref,
    names_ref,
    near_ref,
):
    near_total = 0
    for chunk in range(CHUNKS):
        reach = (nbr_ref[:, chunk * 128 : (chunk + 1) * 128] - (chunk * 128 - 64)) & (GRAINS - 1)
        near_one = (jnp.max(reach.astype(jnp.float32)) < 256.0).astype(jnp.int32)
        near_ref[chunk] = near_one
        near_total = near_total + near_one
    all_near = near_total == CHUNKS

    tiles = strain_rows((disp_ref, upper_ref), dup_ref)
    for point in range(4):
        for comp in range(6):
            start = comp * 32 + point * 8
            strain_ref[start : start + 8, :] = tiles[point][comp]
    strain_ref[192:256, :] = jnp.zeros((64, 128), jnp.float32)

    for row in range(32):
        value = strain_ref[pl.ds(row, 8, stride=32), :]
        high = value.astype(jnp.bfloat16)
        split_high_ref[:, row * 128 : (row + 1) * 128] = high
        split_low_ref[:, row * 128 : (row + 1) * 128] = (value - high.astype(jnp.float32)).astype(
            jnp.bfloat16
        )
    sel = sel_ref[...]
    slot_strain = lax.dot_general(
        sel, split_high_ref[...], NT, preferred_element_type=jnp.float32
    ) + lax.dot_general(sel, split_low_ref[...], NT, preferred_element_type=jnp.float32)
    columns = [
        [
            jnp.broadcast_to(slot_strain[group * 8 : (group + 1) * 8, comp : comp + 1], (8, 128))
            for comp in range(6)
        ]
        for group in range(GROUPS)
    ]
    strain_t = lax.dot_general(
        split_high_ref[...], sel, NT, preferred_element_type=jnp.float32
    ) + lax.dot_general(split_low_ref[...], sel, NT, preferred_element_type=jnp.float32)
    sums_ref[...] = jnp.zeros((192, 128), jnp.float32)

    def first_step(chunk, carry):
        lanes = lanes_of(chunk)
        block = lax.broadcasted_iota(jnp.int32, (16, 128), 0).astype(jnp.float32)
        for contact in range(CONTACTS):
            names = jnp.broadcast_to(nbr_ref[contact : contact + 1, lanes], (16, 128))
            wanted = (names & 127) + jnp.where((names >> 7) == chunk, 0, 128)
            wanted = (wanted.astype(jnp.float32) - block).astype(jnp.bfloat16)
            onehot_ref[chunk * CONTACTS + contact] = jnp.concatenate(
                [
                    jnp.where(wanted == jnp.bfloat16(part * 16), jnp.bfloat16(1), jnp.bfloat16(0))
                    for part in range(16)
                ],
                axis=0,
            )
        for pair in range(0, GROUPS, 2):
            groups = (pair, pair + 1)
            totals = {}
            for contact in range(CONTACTS):
                basis = [row8(lp_ref.at[comp], contact, lanes) for comp in range(6)]
                normal = [row8(nrm_ref.at[axis_id], contact, lanes) for axis_id in range(3)]
                for group in groups:
                    rows = slice(group * 8, (group + 1) * 8)
                    affine = columns[group][0] * basis[0]
                    for comp in range(1, 6):
                        affine = affine + columns[group][comp] * basis[comp]
                    force = wt_ref[contact, rows, lanes] * affine
                    for axis_id in range(3):
                        term = force * normal[axis_id]
                        key = (group, axis_id)
                        totals[key] = totals[key] + term if contact else term
            for group in groups:
                factor = cd_ref[group * 8 : (group + 1) * 8, lanes]
                for axis_id in range(3):
                    start = axis_id * 32 + group * 8
                    first_ref[start : start + 8, lanes] = factor * totals[group, axis_id]
        return carry

    lax.fori_loop(0, CHUNKS, first_step, 0)

    half = lax.broadcasted_iota(jnp.int32, (8, 128), 1) < 64

    def gather_near(source_ref, chunk, moved_ref):
        lanes = lanes_of(chunk)
        lanes_up = lanes_of((chunk + 1) & (CHUNKS - 1))
        lanes_down = lanes_of((chunk + CHUNKS - 1) & (CHUNKS - 1))
        tiles = [slice(tile * 8, (tile + 1) * 8) for tile in range(12)]
        own = [source_ref[tile, lanes] for tile in tiles]
        sides = [
            jnp.where(half, source_ref[tile, lanes_up], source_ref[tile, lanes_down])
            for tile in tiles
        ]
        for contact in range(CONTACTS):
            names = row8(nbr_ref, contact, lanes)
            index = names & 127
            inside = (names >> 7) == chunk
            for place, tile in enumerate(tiles):
                moved_ref[tile, contact * 128 : (contact + 1) * 128] = jnp.where(
                    inside, take_lanes(own[place], index), take_lanes(sides[place], index)
                )

    tall = lax.broadcasted_iota(jnp.int32, (96, 128), 1) < 64

    def dot_pieces(source_ref, chunk, exact):
        lanes = lanes_of(chunk)
        lanes_up = lanes_of((chunk + 1) & (CHUNKS - 1))
        lanes_down = lanes_of((chunk + CHUNKS - 1) & (CHUNKS - 1))
        own = source_ref[:, lanes]
        sides = jnp.where(tall, source_ref[:, lanes_up], source_ref[:, lanes_down])
        window = jnp.concatenate([own, sides], axis=1)
        high = window.astype(jnp.bfloat16)
        if exact:
            low = (window - high.astype(jnp.float32)).astype(jnp.bfloat16)
            both = jnp.concatenate([high, low], axis=0)

        def pieces(pair):
            place = chunk * CONTACTS + 2 * pair
            picks = jnp.concatenate([onehot_ref[place], onehot_ref[place + 1]], axis=1)
            if not exact:
                return jnp.dot(high, picks, preferred_element_type=jnp.float32)
            value = jnp.dot(both, picks, preferred_element_type=jnp.float32)
            return value[0:96] + value[96:192]

        return pieces

    def scratch_pieces(moved_ref):
        return lambda pair: moved_ref[:, pair * 256 : (pair + 1) * 256]

    def chunk_forces(source_ref, chunk, pieces, use):
        lanes = lanes_of(chunk)
        own = [source_ref[tile * 8 : (tile + 1) * 8, lanes] for tile in range(12)]
        for pair in range(CONTACTS // 2):
            moved = pieces(pair)
            for half_id in range(2):
                contact = 2 * pair + half_id
                columns_of = slice(half_id * 128, (half_id + 1) * 128)
                normal = [row8(nrm_ref.at[axis_id], contact, lanes) for axis_id in range(3)]
                for group in range(GROUPS):
                    stretch = None
                    for axis_id in range(3):
                        tile = axis_id * 4 + group
                        there = moved[tile * 8 : (tile + 1) * 8, columns_of]
                        term = normal[axis_id] * (there - own[tile])
                        stretch = term if stretch is None else stretch + term
                    rows = slice(group * 8, (group + 1) * 8)
                    use(contact, group, wt_ref[contact, rows, lanes] * stretch, normal)
        return own

    def gather_far(source_ref, chunk, moved_ref):
        lanes = lanes_of(chunk)
        for contact in range(CONTACTS):
            names_ref[contact] = row8(nbr_ref, contact, lanes)

        def contact_step(contact, carry):
            names = names_ref[contact]
            index = names & 127
            block = names >> 7

            def step(place, values):
                hit = block == place
                return tuple(
                    jnp.where(
                        hit,
                        take_lanes(source_ref[tile * 8 : (tile + 1) * 8, lanes_of(place)], index),
                        values[tile],
                    )
                    for tile in range(12)
                )

            zero = jnp.zeros((8, 128), jnp.float32)
            values = lax.fori_loop(0, CHUNKS, step, (zero,) * 12)
            for tile in range(12):
                moved_ref[tile * 8 : (tile + 1) * 8, lanes_of(contact)] = values[tile]
            return carry

        lax.fori_loop(0, CONTACTS, contact_step, 0)

    def all_chunks(source_ref, work, exact):
        unroll = 4 if exact else 8

        @pl.when(all_near)
        def _():
            def step(turn, carry):
                for place in range(unroll):
                    chunk = turn * unroll + place
                    work(chunk, dot_pieces(source_ref, chunk, exact))
                return carry

            lax.fori_loop(0, CHUNKS // unroll, step, 0)

        @pl.when(jnp.logical_not(all_near))
        def _():
            def step(chunk, carry):
                near = near_ref[chunk] == 1

                @pl.when(near)
                def _():
                    gather_near(source_ref, chunk, moved_ref)

                @pl.when(jnp.logical_not(near))
                def _():
                    gather_far(source_ref, chunk, moved_ref)

                work(chunk, scratch_pieces(moved_ref))
                return carry

            lax.fori_loop(0, CHUNKS, step, 0)

    def sweep(source_ref, target_ref):
        def work(chunk, pieces):
            totals = [None] * 12

            def use(contact, group, force, normal):
                for axis_id in range(3):
                    tile = axis_id * 4 + group
                    term = force * normal[axis_id]
                    totals[tile] = totals[tile] + term if contact else term

            own = chunk_forces(source_ref, chunk, pieces, use)
            lanes = lanes_of(chunk)
            for group in range(GROUPS):
                factor = cd_ref[group * 8 : (group + 1) * 8, lanes]
                for axis_id in range(3):
                    tile = axis_id * 4 + group
                    rows = slice(tile * 8, (tile + 1) * 8)
                    target_ref[rows, lanes] = own[tile] + first_ref[rows, lanes] + factor * totals[tile]

        all_chunks(source_ref, work, EXACT)

    def stress_work(chunk, pieces):
        lanes = lanes_of(chunk)
        totals = [None] * 24

        def use(contact, group, force, normal):
            for comp in range(6):
                tile = comp * 4 + group
                term = force * row8(lp_ref.at[comp], contact, lanes)
                totals[tile] = totals[tile] + term if contact else term

        chunk_forces(current, chunk, pieces, use)
        for tile in range(24):
            sums_ref[tile * 8 : (tile + 1) * 8, :] += totals[tile]

    current = first_ref
    for turn in range(SWEEPS - 1):
        target = fluct_b_ref if turn % 2 else fluct_a_ref
        sweep(current, target)
        current = target
    all_chunks(current, stress_work, True)

    lane32 = lax.broadcasted_iota(jnp.int32, (32, 128), 1)
    table = jnp.zeros((32, 128), jnp.float32)
    for comp in range(6):
        total = jnp.sum(sums_ref[comp * 32 : (comp + 1) * 32, :], axis=1, keepdims=True)
        table = jnp.where(lane32 == comp, total * (1.0 / GRAINS), table)
    full = jnp.concatenate([table, jnp.zeros((96, 128), jnp.float32)], axis=0)
    shares = []
    for row_id in range(6):
        share = None
        for col_id in range(6):
            where = PAIRS.index((min(row_id, col_id), max(row_id, col_id)))
            term = tan_ref[where : where + 1, :] * strain_t[col_id : col_id + 1, :]
            share = term if share is None else share + term
        shares.append(share)
    flipped = jnp.transpose(full)[0:6, 0:32] + jnp.concatenate(shares, axis=0)
    band_ref[...] = flipped
    dup_ref[0:6, 0:32] = flipped

    strain = [strain_ref[comp * 32 : (comp + 1) * 32, :] for comp in range(6)]
    rank = rank_ref[...]
    banded = rank >= 0
    place = jnp.maximum(rank, 0)
    stress = []
    for row_id in range(6):
        running = None
        for col_id in range(6):
            where = PAIRS.index((min(row_id, col_id), max(row_id, col_id)))
            term = (
                tangent_ref[where * 32 : (where + 1) * 32, :].astype(jnp.float32) * strain[col_id]
            )
            running = term if running is None else running + term
        values = take_lanes(jnp.broadcast_to(dup_ref[row_id : row_id + 1, :], (32, 128)), place)
        value = jnp.where(banded, values, running)
        stress_ref[row_id * 32 : (row_id + 1) * 32, :] = value
        stress.append(value)
    planes = force_rows(
        [[stress[comp][point * 8 : (point + 1) * 8, :] for comp in range(6)] for point in range(4)]
    )
    for axis_id in range(3):
        pre_ref[axis_id] = load_ref[axis_id] - planes[0][axis_id][0:4]
        carried_ref[axis_id] = planes[1][axis_id][0:4]


VMEM = pl.BlockSpec(memory_space=pltpu.VMEM)
HBM = pl.BlockSpec(memory_space=pltpu.HBM)


def run_template(
    flags, stiffness, normals, branch_length, neighbours, displacement, load, elastic_tangent
):
    f32 = jnp.float32
    kept = [normals, neighbours, displacement, load, elastic_tangent]
    return pl.pallas_call(
        template_kernel,
        out_shape=(
            jax.ShapeDtypeStruct((CONTACTS, SLOT_COUNT, GRAINS), f32),
            jax.ShapeDtypeStruct((SLOT_COUNT, GRAINS), f32),
            jax.ShapeDtypeStruct((21, SLOT_COUNT), f32),
            jax.ShapeDtypeStruct((21, SLOT_COUNT), f32),
            jax.ShapeDtypeStruct((32, 128), jnp.int32),
            jax.ShapeDtypeStruct((SLOT_COUNT, 4096), jnp.bfloat16),
            jax.ShapeDtypeStruct((6, CONTACTS, GRAINS), f32),
        )
        + tuple(jax.ShapeDtypeStruct(value.shape, value.dtype) for value in kept),
        in_specs=[HBM] * 8,
        out_specs=(VMEM,) * 12,
        scratch_shapes=[
            pltpu.VMEM((SLOT_COUNT * CONTACTS, 128), f32),
            pltpu.VMEM((256, 128), f32),
            pltpu.VMEM((CONTACTS, 64, GRAINS), jnp.bfloat16),
            pltpu.VMEM((32, 128), jnp.int32),
            pltpu.VMEM((SLOT_COUNT, CONTACTS, GRAINS), jnp.bfloat16),
            pltpu.VMEM((CONTACTS, GRAINS), f32),
            pltpu.SemaphoreType.DMA((7,)),
            pltpu.SemaphoreType.DMA((4,)),
        ],
        cost_estimate=pl.CostEstimate(flops=40_000_000, bytes_accessed=8_000_000, transcendentals=0),
        compiler_params=pltpu.CompilerParams(vmem_limit_bytes=16 * 1024 * 1024),
        name="template",
    )(
        *[
            pltpu.with_memory_space_constraint(value, pltpu.HBM)
            for value in (flags, stiffness, *kept[:1], branch_length, *kept[1:])
        ]
    )


def run_relax(disp, upper, load, tangent, rank, sel, wt, cd, lp, normals, neighbours, tan):
    f32 = jnp.float32
    return pl.pallas_call(
        relax_kernel,
        out_shape=(
            jax.ShapeDtypeStruct((3, 4, 128), f32),
            jax.ShapeDtypeStruct((3, 4, 128), f32),
            jax.ShapeDtypeStruct((192, 128), f32),
            jax.ShapeDtypeStruct((6, SLOT_COUNT), f32),
        ),
        in_specs=[VMEM] * 12,
        out_specs=(VMEM,) * 4,
        scratch_shapes=[
            pltpu.VMEM((8, 128), f32),
            pltpu.VMEM((256, 128), f32),
            pltpu.VMEM((8, 4096), jnp.bfloat16),
            pltpu.VMEM((8, 4096), jnp.bfloat16),
            pltpu.VMEM((96, GRAINS), f32),
            pltpu.VMEM((96, GRAINS), f32),
            pltpu.VMEM((96, GRAINS), f32),
            pltpu.VMEM((192, 128), f32),
            pltpu.VMEM((CHUNKS * CONTACTS, 256, 128), jnp.bfloat16),
            pltpu.VMEM((96, CONTACTS * 128), f32),
            pltpu.VMEM((CONTACTS, 8, 128), jnp.int32),
            pltpu.SMEM((CHUNKS,), jnp.int32),
        ],
        cost_estimate=pl.CostEstimate(
            flops=200_000_000, bytes_accessed=8_000_000, transcendentals=0
        ),
        compiler_params=pltpu.CompilerParams(vmem_limit_bytes=28 * 1024 * 1024),
        name="relax",
    )(disp, upper, load, tangent, rank, sel, wt, cd, lp, normals, neighbours, tan)


def body(
    displacement,
    load,
    elastic_tangent,
    band_flags,
    contact_stiffness,
    normals,
    branch_length,
    neighbours,
):
    upper = shifted(displacement, ("row", "col"), -1)
    wt, cd, tangent, tan, rank, sel, lp, nrm, nbr, disp, load_here, elastic = run_template(
        band_flags.reshape(32, 128),
        contact_stiffness,
        normals,
        branch_length,
        neighbours,
        displacement.reshape(3, 4, 128),
        load.reshape(3, 4, 128),
        elastic_tangent.reshape(672, 128),
    )
    pre, carried, stress, band = run_relax(
        disp, upper.reshape(3, 4, 128), load_here, elastic, rank, sel, wt, cd, lp, nrm, nbr, tan
    )
    arrived = shifted(carried, ("row", "col"), 1)
    residual = (pre - arrived).reshape(3, 1, 4, 128)
    return (residual, stress.reshape(6, 8, 1, 4, 128), tangent, band)


def solution(mesh):
    placed = (
        P(None, ("row", "col"), None, None),
        P(None, ("row", "col"), None, None),
        P(None, None, ("row", "col"), None, None),
        P(None, ("row", "col"), None, None),
        P(("row", "col"), None, None),
        P(),
        P(),
        P(),
    )
    return jax.shard_map(
        body,
        mesh=mesh,
        in_specs=placed,
        out_specs=(
            P(None, ("row", "col"), None, None),
            P(None, None, ("row", "col"), None, None),
            P(None, ("row", "col")),
            P(None, ("row", "col")),
        ),
        check_vma=False,
    )
```

```python
import jax
import jax.numpy as jnp
import numpy as np
from jax import lax
from jax.experimental import pallas as pl
from jax.experimental.pallas import tpu as pltpu
from jax.sharding import PartitionSpec as P

SWEEPS = 4
RELAX_FACTOR = 0.8
LOW = float(0.5 - 0.5 / np.sqrt(3.0))
HIGH = float(0.5 + 0.5 / np.sqrt(3.0))
GRAINS = 2048
CONTACTS = 8
SLOT_COUNT = 32
GROUPS = SLOT_COUNT // 8
CHUNKS = GRAINS // 128
UNROLL = 4
EXACT = False
PAIRS = [(row_id, col_id) for row_id in range(6) for col_id in range(row_id, 6)]
NT = (((1,), (1,)), ((), ()))


def shifted(value, axis, steps):
    count = lax.axis_size(axis)
    leading, last = (max(0, -steps), min(count, count - steps))
    return lax.ppermute(value, axis, [(source, source + steps) for source in range(leading, last)])


def lanes_of(chunk):
    return pl.ds(pl.multiple_of(chunk * 128, 128), 128)


def row8(ref, row, lanes):
    return jnp.broadcast_to(ref[row : row + 1, lanes], (8, 128))


LANE_GATHER = lax.GatherDimensionNumbers(
    offset_dims=(),
    collapsed_slice_dims=(1,),
    start_index_map=(1,),
    operand_batching_dims=(0,),
    start_indices_batching_dims=(0,),
)


def take_lanes(table, index):
    return lax.gather(
        table,
        index[..., None],
        LANE_GATHER,
        slice_sizes=(1, 1),
        mode=lax.GatherScatterMode.PROMISE_IN_BOUNDS,
    )


def template_kernel(
    flags_hbm,
    stiff_hbm,
    nrm_hbm,
    br_hbm,
    nbr_hbm,
    disp_hbm,
    load_hbm,
    tangent_hbm,
    wt_ref,
    cd_ref,
    tan_ref,
    rank_ref,
    sel_ref,
    lp_ref,
    nrm_ref,
    nbr_ref,
    disp_ref,
    load_ref,
    tangent_ref,
    raw_ref,
    basis_ref,
    split_ref,
    flags_ref,
    stiff_ref,
    br_ref,
    small_sems,
    stiff_sems,
):
    small = [
        pltpu.make_async_copy(source, target, small_sems.at[place])
        for place, (source, target) in enumerate(
            [
                (flags_hbm, flags_ref),
                (nrm_hbm, nrm_ref),
                (br_hbm, br_ref),
                (nbr_hbm, nbr_ref),
                (disp_hbm, disp_ref),
                (load_hbm, load_ref),
                (tangent_hbm, tangent_ref),
            ]
        )
    ]
    quarter = GRAINS // 4
    big = [
        pltpu.make_async_copy(
            stiff_hbm.at[:, :, pl.ds(part * quarter, quarter)],
            stiff_ref.at[:, :, pl.ds(part * quarter, quarter)],
            stiff_sems.at[part],
        )
        for part in range(4)
    ]
    for copy in small[:4] + big + small[4:]:
        copy.start()
    for copy in small[:4]:
        copy.wait()

    flags = flags_ref[...]
    flags_f = flags.astype(jnp.float32)
    tri = (
        lax.broadcasted_iota(jnp.int32, (128, 128), 0)
        <= lax.broadcasted_iota(jnp.int32, (128, 128), 1)
    ).astype(jnp.float32)
    inside = jnp.dot(flags_f, tri, preferred_element_type=jnp.float32)
    before = (
        lax.broadcasted_iota(jnp.int32, (32, 32), 1) < lax.broadcasted_iota(jnp.int32, (32, 32), 0)
    ).astype(jnp.float32)
    ahead = jnp.sum(
        jnp.dot(before, flags_f, preferred_element_type=jnp.float32), axis=1, keepdims=True
    )
    rank = jnp.where(flags == 1, (inside + ahead - 1.0).astype(jnp.int32), -1)
    rank_ref[...] = rank
    live_total = jnp.sum(flags_f)
    slot_rows = lax.broadcasted_iota(jnp.int32, (32, 128), 0)
    for row in range(32):
        picked = jnp.broadcast_to(rank_ref[row : row + 1, :], (32, 128)) == slot_rows
        sel_ref[:, row * 128 : (row + 1) * 128] = jnp.where(picked, 1.0, 0.0).astype(jnp.bfloat16)

    basis_ref[168:256, :] = jnp.zeros((88, 128), jnp.float32)

    def chunk_step(chunk, carry):
        lanes = lanes_of(chunk)
        names = nbr_ref[:, lanes]
        own = lax.broadcasted_iota(jnp.int32, (8, 128), 1) + chunk * 128
        mask = jnp.where(names != own, 1.0, 0.0)
        n0, n1, n2 = (nrm_ref[axis_id, :, lanes] for axis_id in range(3))
        length = br_ref[:, lanes]
        proj = [n0 * n0, n1 * n1, n2 * n2, n1 * n2, n0 * n2, n0 * n1]
        scaled = [length * value for value in proj]
        for comp in range(6):
            lp_ref[comp, :, lanes] = scaled[comp]
        for place, (row_id, col_id) in enumerate(PAIRS):
            basis_ref[place * 8 : (place + 1) * 8, :] = scaled[row_id] * scaled[col_id]
        for contact in range(CONTACTS):
            basis = basis_ref[pl.ds(contact, 32, stride=8), :]
            high = basis.astype(jnp.bfloat16)
            split_ref[contact, 0:32, lanes] = high
            split_ref[contact, 32:64, lanes] = (basis - high.astype(jnp.float32)).astype(
                jnp.bfloat16
            )
        for slot in range(SLOT_COUNT):
            raw_ref[slot * 8 : (slot + 1) * 8, :] = (
                stiff_ref[slot, :, lanes].astype(jnp.float32) * mask
            )
        for group in range(GROUPS):
            total = None
            for contact in range(CONTACTS):
                value = raw_ref[pl.ds(group * 64 + contact, 8, stride=8), :]
                wt_ref[contact, group * 8 : (group + 1) * 8, lanes] = value
                total = value if total is None else total + value
            cd_ref[group * 8 : (group + 1) * 8, lanes] = RELAX_FACTOR / total
        return carry

    for part in range(4):
        big[part].wait()
        lax.fori_loop(part * CHUNKS // 4, (part + 1) * CHUNKS // 4, chunk_step, 0)

    acc = jnp.zeros((64, 32), jnp.float32)
    for contact in range(CONTACTS):
        weights = wt_ref[contact].astype(jnp.bfloat16)
        acc = acc + lax.dot_general(
            split_ref[contact], weights, NT, preferred_element_type=jnp.float32
        )
    acc = acc[0:32] + acc[32:64]
    slot_lane = lax.broadcasted_iota(jnp.int32, (32, 32), 1).astype(jnp.float32)
    acc = jnp.where(slot_lane < live_total, acc * (1.0 / GRAINS), 0.0)
    tan_ref[...] = acc[:21]
    for copy in small[4:]:
        copy.wait()


def lerp(low_value, high_value, bit):
    weight = HIGH if bit else LOW
    return low_value + weight * (high_value - low_value)


def strain_rows(plane_refs, dup_ref):
    row = lax.broadcasted_iota(jnp.int32, (8, 128), 0)
    lane = lax.broadcasted_iota(jnp.int32, (8, 128), 1)
    z_weight = jnp.where(row < 4, LOW, HIGH)
    last_y = (row & 3) == 3
    last_z = lane == 127
    gradient = {}
    for axis_id in range(3):
        along, slope = {}, {}
        for bit_x in range(2):
            plane = plane_refs[bit_x][axis_id]
            dup_ref[0:4, :] = plane
            dup_ref[4:8, :] = plane
            base = dup_ref[...]
            for bit_y in range(2):
                value = base if bit_y == 0 else jnp.where(last_y, 0.0, pltpu.roll(base, 7, 0))
                after = jnp.where(last_z, 0.0, pltpu.roll(value, 127, 1))
                slope[bit_x, bit_y] = after - value
                along[bit_x, bit_y] = value + z_weight * (after - value)
        for gauss_y in range(2):
            for gauss_x in range(2):
                point = 2 * gauss_x + gauss_y
                face = [lerp(along[bit_x, 0], along[bit_x, 1], gauss_y) for bit_x in range(2)]
                gradient[point, axis_id, 0] = face[1] - face[0]
                gradient[point, axis_id, 1] = lerp(
                    along[0, 1] - along[0, 0], along[1, 1] - along[1, 0], gauss_x
                )
                edge = [lerp(slope[bit_x, 0], slope[bit_x, 1], gauss_y) for bit_x in range(2)]
                gradient[point, axis_id, 2] = lerp(edge[0], edge[1], gauss_x)
    return [
        [
            gradient[point, 0, 0],
            gradient[point, 1, 1],
            gradient[point, 2, 2],
            gradient[point, 1, 2] + gradient[point, 2, 1],
            gradient[point, 0, 2] + gradient[point, 2, 0],
            gradient[point, 0, 1] + gradient[point, 1, 0],
        ]
        for point in range(4)
    ]


def weigh(low_value, high_value, corner_bit):
    if corner_bit:
        return LOW * low_value + HIGH * high_value
    return HIGH * low_value + LOW * high_value


def force_rows(stress):
    row = lax.broadcasted_iota(jnp.int32, (8, 128), 0)
    lane = lax.broadcasted_iota(jnp.int32, (8, 128), 1)
    z_high = jnp.where(row < 4, LOW, HIGH)
    z_low = jnp.where(row < 4, HIGH, LOW)
    voigt = [[0, 5, 4], [5, 1, 3], [4, 3, 2]]
    planes = [[None] * 3, [None] * 3]
    for axis_id in range(3):
        part = [[stress[point][voigt[axis_id][other]] for point in range(4)] for other in range(3)]
        flow = [part[0][gauss_y] + part[0][2 + gauss_y] for gauss_y in range(2)]
        for bit_x in range(2):
            side_y = [weigh(part[1][gauss_y], part[1][2 + gauss_y], bit_x) for gauss_y in range(2)]
            side_z = [weigh(part[2][gauss_y], part[2][2 + gauss_y], bit_x) for gauss_y in range(2)]
            total_y = side_y[0] + side_y[1]
            total = None
            for bit_y in range(2):
                first = weigh(flow[0], flow[1], bit_y)
                first = first if bit_x else -first
                first = first + total_y if bit_y else first - total_y
                second = weigh(side_z[0], side_z[1], bit_y)
                near = z_low * first - second
                far = z_high * first + second
                far = jnp.where(lane == 0, 0.0, pltpu.roll(far, 1, 1))
                both = near + far
                both = both + pltpu.roll(both, 4, 0)
                if bit_y:
                    both = jnp.where((row & 3) == 0, 0.0, pltpu.roll(both, 1, 0))
                total = both if total is None else total + both
            planes[bit_x][axis_id] = 0.125 * total
    return planes


def relax_kernel(
    disp_ref,
    upper_ref,
    tangent_ref,
    rank_ref,
    sel_ref,
    wt_ref,
    cd_ref,
    lp_ref,
    nrm_ref,
    nbr_ref,
    tan_ref,
    carried_ref,
    stress_ref,
    band_ref,
    dup_ref,
    strain_ref,
    split_high_ref,
    split_low_ref,
    first_ref,
    fluct_a_ref,
    fluct_b_ref,
    sums_ref,
    onehot_ref,
    moved_ref,
    names_ref,
    near_ref,
):
    near_total = 0
    for chunk in range(CHUNKS):
        reach = (nbr_ref[:, chunk * 128 : (chunk + 1) * 128] - (chunk * 128 - 64)) & (GRAINS - 1)
        near_one = (jnp.max(reach.astype(jnp.float32)) < 256.0).astype(jnp.int32)
        near_ref[chunk] = near_one
        near_total = near_total + near_one
    all_near = near_total == CHUNKS

    tiles = strain_rows((disp_ref, upper_ref), dup_ref)
    for point in range(4):
        for comp in range(6):
            start = comp * 32 + point * 8
            strain_ref[start : start + 8, :] = tiles[point][comp]
    strain_ref[192:256, :] = jnp.zeros((64, 128), jnp.float32)

    for row in range(32):
        value = strain_ref[pl.ds(row, 8, stride=32), :]
        high = value.astype(jnp.bfloat16)
        split_high_ref[:, row * 128 : (row + 1) * 128] = high
        split_low_ref[:, row * 128 : (row + 1) * 128] = (value - high.astype(jnp.float32)).astype(
            jnp.bfloat16
        )
    sel = sel_ref[...]
    slot_strain = lax.dot_general(
        sel, split_high_ref[...], NT, preferred_element_type=jnp.float32
    ) + lax.dot_general(sel, split_low_ref[...], NT, preferred_element_type=jnp.float32)
    columns = [
        [
            jnp.broadcast_to(slot_strain[group * 8 : (group + 1) * 8, comp : comp + 1], (8, 128))
            for comp in range(6)
        ]
        for group in range(GROUPS)
    ]
    strain_t = lax.dot_general(
        split_high_ref[...], sel, NT, preferred_element_type=jnp.float32
    ) + lax.dot_general(split_low_ref[...], sel, NT, preferred_element_type=jnp.float32)
    sums_ref[...] = jnp.zeros((192, 128), jnp.float32)

    def first_step(chunk, carry):
        lanes = lanes_of(chunk)
        block = lax.broadcasted_iota(jnp.int32, (16, 128), 0).astype(jnp.float32)
        for contact in range(CONTACTS):
            names = jnp.broadcast_to(nbr_ref[contact : contact + 1, lanes], (16, 128))
            wanted = (names & 127) + jnp.where((names >> 7) == chunk, 0, 128)
            wanted = (wanted.astype(jnp.float32) - block).astype(jnp.bfloat16)
            onehot_ref[chunk * CONTACTS + contact] = jnp.concatenate(
                [
                    jnp.where(wanted == jnp.bfloat16(part * 16), jnp.bfloat16(1), jnp.bfloat16(0))
                    for part in range(16)
                ],
                axis=0,
            )
        for pair in range(0, GROUPS, 2):
            groups = (pair, pair + 1)
            totals = {}
            for contact in range(CONTACTS):
                basis = [row8(lp_ref.at[comp], contact, lanes) for comp in range(6)]
                normal = [row8(nrm_ref.at[axis_id], contact, lanes) for axis_id in range(3)]
                for group in groups:
                    rows = slice(group * 8, (group + 1) * 8)
                    affine = columns[group][0] * basis[0]
                    for comp in range(1, 6):
                        affine = affine + columns[group][comp] * basis[comp]
                    force = wt_ref[contact, rows, lanes] * affine
                    for axis_id in range(3):
                        term = force * normal[axis_id]
                        key = (group, axis_id)
                        totals[key] = totals[key] + term if contact else term
            for group in groups:
                factor = cd_ref[group * 8 : (group + 1) * 8, lanes]
                for axis_id in range(3):
                    start = axis_id * 32 + group * 8
                    first_ref[start : start + 8, lanes] = factor * totals[group, axis_id]
        return carry

    lax.fori_loop(0, CHUNKS, first_step, 0)

    half = lax.broadcasted_iota(jnp.int32, (8, 128), 1) < 64

    def gather_near(source_ref, chunk, moved_ref):
        lanes = lanes_of(chunk)
        lanes_up = lanes_of((chunk + 1) & (CHUNKS - 1))
        lanes_down = lanes_of((chunk + CHUNKS - 1) & (CHUNKS - 1))
        tiles = [slice(tile * 8, (tile + 1) * 8) for tile in range(12)]
        own = [source_ref[tile, lanes] for tile in tiles]
        sides = [
            jnp.where(half, source_ref[tile, lanes_up], source_ref[tile, lanes_down])
            for tile in tiles
        ]
        for contact in range(CONTACTS):
            names = row8(nbr_ref, contact, lanes)
            index = names & 127
            inside = (names >> 7) == chunk
            for place, tile in enumerate(tiles):
                moved_ref[tile, contact * 128 : (contact + 1) * 128] = jnp.where(
                    inside, take_lanes(own[place], index), take_lanes(sides[place], index)
                )

    tall = lax.broadcasted_iota(jnp.int32, (96, 128), 1) < 64

    def dot_pieces(source_ref, chunk, exact):
        lanes = lanes_of(chunk)
        lanes_up = lanes_of((chunk + 1) & (CHUNKS - 1))
        lanes_down = lanes_of((chunk + CHUNKS - 1) & (CHUNKS - 1))
        own = source_ref[:, lanes]
        sides = jnp.where(tall, source_ref[:, lanes_up], source_ref[:, lanes_down])
        window = jnp.concatenate([own, sides], axis=1)
        high = window.astype(jnp.bfloat16)
        if exact:
            low = (window - high.astype(jnp.float32)).astype(jnp.bfloat16)
            both = jnp.concatenate([high, low], axis=0)

        def pieces(pair):
            place = chunk * CONTACTS + 2 * pair
            picks = jnp.concatenate([onehot_ref[place], onehot_ref[place + 1]], axis=1)
            if not exact:
                return jnp.dot(high, picks, preferred_element_type=jnp.float32)
            value = jnp.dot(both, picks, preferred_element_type=jnp.float32)
            return value[0:96] + value[96:192]

        return pieces

    def scratch_pieces(moved_ref):
        return lambda pair: moved_ref[:, pair * 256 : (pair + 1) * 256]

    def chunk_forces(source_ref, chunk, pieces, use):
        lanes = lanes_of(chunk)
        own = [source_ref[tile * 8 : (tile + 1) * 8, lanes] for tile in range(12)]
        for pair in range(CONTACTS // 2):
            moved = pieces(pair)
            for half_id in range(2):
                contact = 2 * pair + half_id
                columns_of = slice(half_id * 128, (half_id + 1) * 128)
                normal = [row8(nrm_ref.at[axis_id], contact, lanes) for axis_id in range(3)]
                for group in range(GROUPS):
                    stretch = None
                    for axis_id in range(3):
                        tile = axis_id * 4 + group
                        there = moved[tile * 8 : (tile + 1) * 8, columns_of]
                        term = normal[axis_id] * (there - own[tile])
                        stretch = term if stretch is None else stretch + term
                    rows = slice(group * 8, (group + 1) * 8)
                    use(contact, group, wt_ref[contact, rows, lanes] * stretch, normal)
        return own

    def gather_far(source_ref, chunk, moved_ref):
        lanes = lanes_of(chunk)
        for contact in range(CONTACTS):
            names_ref[contact] = row8(nbr_ref, contact, lanes)

        def contact_step(contact, carry):
            names = names_ref[contact]
            index = names & 127
            block = names >> 7

            def step(place, values):
                hit = block == place
                return tuple(
                    jnp.where(
                        hit,
                        take_lanes(source_ref[tile * 8 : (tile + 1) * 8, lanes_of(place)], index),
                        values[tile],
                    )
                    for tile in range(12)
                )

            zero = jnp.zeros((8, 128), jnp.float32)
            values = lax.fori_loop(0, CHUNKS, step, (zero,) * 12)
            for tile in range(12):
                moved_ref[tile * 8 : (tile + 1) * 8, lanes_of(contact)] = values[tile]
            return carry

        lax.fori_loop(0, CONTACTS, contact_step, 0)

    def all_chunks(source_ref, work, exact):
        unroll = 4 if exact else 8

        @pl.when(all_near)
        def _():
            def step(turn, carry):
                for place in range(unroll):
                    chunk = turn * unroll + place
                    work(chunk, dot_pieces(source_ref, chunk, exact))
                return carry

            lax.fori_loop(0, CHUNKS // unroll, step, 0)

        @pl.when(jnp.logical_not(all_near))
        def _():
            def step(chunk, carry):
                near = near_ref[chunk] == 1

                @pl.when(near)
                def _():
                    gather_near(source_ref, chunk, moved_ref)

                @pl.when(jnp.logical_not(near))
                def _():
                    gather_far(source_ref, chunk, moved_ref)

                work(chunk, scratch_pieces(moved_ref))
                return carry

            lax.fori_loop(0, CHUNKS, step, 0)

    def sweep(source_ref, target_ref):
        def work(chunk, pieces):
            totals = [None] * 12

            def use(contact, group, force, normal):
                for axis_id in range(3):
                    tile = axis_id * 4 + group
                    term = force * normal[axis_id]
                    totals[tile] = totals[tile] + term if contact else term

            own = chunk_forces(source_ref, chunk, pieces, use)
            lanes = lanes_of(chunk)
            for group in range(GROUPS):
                factor = cd_ref[group * 8 : (group + 1) * 8, lanes]
                for axis_id in range(3):
                    tile = axis_id * 4 + group
                    rows = slice(tile * 8, (tile + 1) * 8)
                    target_ref[rows, lanes] = own[tile] + first_ref[rows, lanes] + factor * totals[tile]

        all_chunks(source_ref, work, EXACT)

    def stress_work(chunk, pieces):
        lanes = lanes_of(chunk)
        totals = [None] * 24

        def use(contact, group, force, normal):
            for comp in range(6):
                tile = comp * 4 + group
                term = force * row8(lp_ref.at[comp], contact, lanes)
                totals[tile] = totals[tile] + term if contact else term

        chunk_forces(current, chunk, pieces, use)
        for tile in range(24):
            sums_ref[tile * 8 : (tile + 1) * 8, :] += totals[tile]

    current = first_ref
    for turn in range(SWEEPS - 1):
        target = fluct_b_ref if turn % 2 else fluct_a_ref
        sweep(current, target)
        current = target
    all_chunks(current, stress_work, True)

    lane32 = lax.broadcasted_iota(jnp.int32, (32, 128), 1)
    table = jnp.zeros((32, 128), jnp.float32)
    for comp in range(6):
        total = jnp.sum(sums_ref[comp * 32 : (comp + 1) * 32, :], axis=1, keepdims=True)
        table = jnp.where(lane32 == comp, total * (1.0 / GRAINS), table)
    full = jnp.concatenate([table, jnp.zeros((96, 128), jnp.float32)], axis=0)
    shares = []
    for row_id in range(6):
        share = None
        for col_id in range(6):
            where = PAIRS.index((min(row_id, col_id), max(row_id, col_id)))
            term = tan_ref[where : where + 1, :] * strain_t[col_id : col_id + 1, :]
            share = term if share is None else share + term
        shares.append(share)
    flipped = jnp.transpose(full)[0:6, 0:32] + jnp.concatenate(shares, axis=0)
    band_ref[...] = flipped
    dup_ref[0:6, 0:32] = flipped

    strain = [strain_ref[comp * 32 : (comp + 1) * 32, :] for comp in range(6)]
    rank = rank_ref[...]
    banded = rank >= 0
    place = jnp.maximum(rank, 0)
    stress = []
    for row_id in range(6):
        running = None
        for col_id in range(6):
            where = PAIRS.index((min(row_id, col_id), max(row_id, col_id)))
            term = (
                tangent_ref[where * 32 : (where + 1) * 32, :].astype(jnp.float32) * strain[col_id]
            )
            running = term if running is None else running + term
        values = take_lanes(jnp.broadcast_to(dup_ref[row_id : row_id + 1, :], (32, 128)), place)
        value = jnp.where(banded, values, running)
        stress_ref[row_id * 32 : (row_id + 1) * 32, :] = value
        stress.append(value)
    planes = force_rows(tiles_of(stress))
    for axis_id in range(3):
        carried_ref[axis_id] = planes[1][axis_id][0:4]


def tiles_of(stress):
    return [
        [stress[comp][point * 8 : (point + 1) * 8, :] for comp in range(6)] for point in range(4)
    ]


def output_kernel(stress_in, band_in, tan_in, load_ref, pre_ref, stress_ref, band_ref, tan_ref):
    stress_ref[...] = stress_in[...]
    band_ref[...] = band_in[...]
    tan_ref[...] = tan_in[...]
    planes = force_rows(tiles_of([stress_in[comp * 32 : (comp + 1) * 32, :] for comp in range(6)]))
    for axis_id in range(3):
        pre_ref[axis_id] = load_ref[axis_id] - planes[0][axis_id][0:4]


VMEM = pl.BlockSpec(memory_space=pltpu.VMEM)
HBM = pl.BlockSpec(memory_space=pltpu.HBM)


def run_template(
    flags, stiffness, normals, branch_length, neighbours, displacement, load, elastic_tangent
):
    f32 = jnp.float32
    kept = [normals, neighbours, displacement, load, elastic_tangent]
    return pl.pallas_call(
        template_kernel,
        out_shape=(
            jax.ShapeDtypeStruct((CONTACTS, SLOT_COUNT, GRAINS), f32),
            jax.ShapeDtypeStruct((SLOT_COUNT, GRAINS), f32),
            jax.ShapeDtypeStruct((21, SLOT_COUNT), f32),
            jax.ShapeDtypeStruct((32, 128), jnp.int32),
            jax.ShapeDtypeStruct((SLOT_COUNT, 4096), jnp.bfloat16),
            jax.ShapeDtypeStruct((6, CONTACTS, GRAINS), f32),
        )
        + tuple(jax.ShapeDtypeStruct(value.shape, value.dtype) for value in kept),
        in_specs=[HBM] * 8,
        out_specs=(VMEM,) * 11,
        scratch_shapes=[
            pltpu.VMEM((SLOT_COUNT * CONTACTS, 128), f32),
            pltpu.VMEM((256, 128), f32),
            pltpu.VMEM((CONTACTS, 64, GRAINS), jnp.bfloat16),
            pltpu.VMEM((32, 128), jnp.int32),
            pltpu.VMEM((SLOT_COUNT, CONTACTS, GRAINS), jnp.bfloat16),
            pltpu.VMEM((CONTACTS, GRAINS), f32),
            pltpu.SemaphoreType.DMA((7,)),
            pltpu.SemaphoreType.DMA((4,)),
        ],
        cost_estimate=pl.CostEstimate(flops=40_000_000, bytes_accessed=8_000_000, transcendentals=0),
        compiler_params=pltpu.CompilerParams(vmem_limit_bytes=16 * 1024 * 1024),
        name="template",
    )(
        *[
            pltpu.with_memory_space_constraint(value, pltpu.HBM)
            for value in (flags, stiffness, *kept[:1], branch_length, *kept[1:])
        ]
    )


def run_relax(disp, upper, tangent, rank, sel, wt, cd, lp, normals, neighbours, tan):
    f32 = jnp.float32
    return pl.pallas_call(
        relax_kernel,
        out_shape=(
            jax.ShapeDtypeStruct((3, 4, 128), f32),
            jax.ShapeDtypeStruct((192, 128), f32),
            jax.ShapeDtypeStruct((6, SLOT_COUNT), f32),
        ),
        in_specs=[VMEM] * 11,
        out_specs=(VMEM,) * 3,
        scratch_shapes=[
            pltpu.VMEM((8, 128), f32),
            pltpu.VMEM((256, 128), f32),
            pltpu.VMEM((8, 4096), jnp.bfloat16),
            pltpu.VMEM((8, 4096), jnp.bfloat16),
            pltpu.VMEM((96, GRAINS), f32),
            pltpu.VMEM((96, GRAINS), f32),
            pltpu.VMEM((96, GRAINS), f32),
            pltpu.VMEM((192, 128), f32),
            pltpu.VMEM((CHUNKS * CONTACTS, 256, 128), jnp.bfloat16),
            pltpu.VMEM((96, CONTACTS * 128), f32),
            pltpu.VMEM((CONTACTS, 8, 128), jnp.int32),
            pltpu.SMEM((CHUNKS,), jnp.int32),
        ],
        cost_estimate=pl.CostEstimate(
            flops=200_000_000, bytes_accessed=8_000_000, transcendentals=0
        ),
        compiler_params=pltpu.CompilerParams(vmem_limit_bytes=28 * 1024 * 1024),
        name="relax",
    )(disp, upper, tangent, rank, sel, wt, cd, lp, normals, neighbours, tan)


def run_output(stress, band, tan, load):
    f32 = jnp.float32
    return pl.pallas_call(
        output_kernel,
        out_shape=(
            jax.ShapeDtypeStruct((3, 4, 128), f32),
            jax.ShapeDtypeStruct((192, 128), f32),
            jax.ShapeDtypeStruct((6, SLOT_COUNT), f32),
            jax.ShapeDtypeStruct((21, SLOT_COUNT), f32),
        ),
        in_specs=[VMEM] * 4,
        out_specs=(VMEM,) * 4,
        cost_estimate=pl.CostEstimate(flops=1_000_000, bytes_accessed=2_000_000, transcendentals=0),
        compiler_params=pltpu.CompilerParams(vmem_limit_bytes=8 * 1024 * 1024),
        name="output",
    )(stress, band, tan, load)


def body(
    displacement,
    load,
    elastic_tangent,
    band_flags,
    contact_stiffness,
    normals,
    branch_length,
    neighbours,
):
    upper = shifted(displacement, ("row", "col"), -1)
    wt, cd, tan, rank, sel, lp, nrm, nbr, disp, load_here, elastic = run_template(
        band_flags.reshape(32, 128),
        contact_stiffness,
        normals,
        branch_length,
        neighbours,
        displacement.reshape(3, 4, 128),
        load.reshape(3, 4, 128),
        elastic_tangent.reshape(672, 128),
    )
    carried, stress_here, band_here = run_relax(
        disp, upper.reshape(3, 4, 128), elastic, rank, sel, wt, cd, lp, nrm, nbr, tan
    )
    arrived = shifted(carried, ("row", "col"), 1)
    pre, stress, band, tangent = run_output(stress_here, band_here, tan, load_here)
    residual = (pre - arrived).reshape(3, 1, 4, 128)
    return (residual, stress.reshape(6, 8, 1, 4, 128), tangent, band)


def solution(mesh):
    placed = (
        P(None, ("row", "col"), None, None),
        P(None, ("row", "col"), None, None),
        P(None, None, ("row", "col"), None, None),
        P(None, ("row", "col"), None, None),
        P(("row", "col"), None, None),
        P(),
        P(),
        P(),
    )
    return jax.shard_map(
        body,
        mesh=mesh,
        in_specs=placed,
        out_specs=(
            P(None, ("row", "col"), None, None),
            P(None, None, ("row", "col"), None, None),
            P(None, ("row", "col")),
            P(None, ("row", "col")),
        ),
        check_vma=False,
    )
```

```python
import jax
import jax.numpy as jnp
import numpy as np
from jax import lax
from jax.experimental import pallas as pl
from jax.experimental.pallas import tpu as pltpu
from jax.sharding import PartitionSpec as P

SWEEPS = 4
RELAX_FACTOR = 0.8
LOW = float(0.5 - 0.5 / np.sqrt(3.0))
HIGH = float(0.5 + 0.5 / np.sqrt(3.0))
GRAINS = 2048
CONTACTS = 8
SLOT_COUNT = 32
GROUPS = SLOT_COUNT // 8
CHUNKS = GRAINS // 128
UNROLL = 4
EXACT = False
PAIRS = [(row_id, col_id) for row_id in range(6) for col_id in range(row_id, 6)]
NT = (((1,), (1,)), ((), ()))


def shifted(value, axis, steps):
    count = lax.axis_size(axis)
    leading, last = (max(0, -steps), min(count, count - steps))
    return lax.ppermute(value, axis, [(source, source + steps) for source in range(leading, last)])


def lanes_of(chunk):
    return pl.ds(pl.multiple_of(chunk * 128, 128), 128)


def row8(ref, row, lanes):
    return jnp.broadcast_to(ref[row : row + 1, lanes], (8, 128))


LANE_GATHER = lax.GatherDimensionNumbers(
    offset_dims=(),
    collapsed_slice_dims=(1,),
    start_index_map=(1,),
    operand_batching_dims=(0,),
    start_indices_batching_dims=(0,),
)


def take_lanes(table, index):
    return lax.gather(
        table,
        index[..., None],
        LANE_GATHER,
        slice_sizes=(1, 1),
        mode=lax.GatherScatterMode.PROMISE_IN_BOUNDS,
    )


def template_kernel(
    flags_hbm,
    stiff_hbm,
    nrm_hbm,
    br_hbm,
    nbr_hbm,
    disp_hbm,
    load_hbm,
    tangent_hbm,
    wt_ref,
    cd_ref,
    tan_ref,
    rank_ref,
    sel_ref,
    lp_ref,
    nrm_ref,
    nbr_ref,
    disp_ref,
    load_ref,
    tangent_ref,
    raw_ref,
    basis_ref,
    split_ref,
    flags_ref,
    stiff_ref,
    br_ref,
    small_sems,
    stiff_sems,
):
    small = [
        pltpu.make_async_copy(source, target, small_sems.at[place])
        for place, (source, target) in enumerate(
            [
                (flags_hbm, flags_ref),
                (nrm_hbm, nrm_ref),
                (br_hbm, br_ref),
                (nbr_hbm, nbr_ref),
                (disp_hbm, disp_ref),
                (load_hbm, load_ref),
                (tangent_hbm, tangent_ref),
            ]
        )
    ]
    quarter = GRAINS // 4
    big = [
        pltpu.make_async_copy(
            stiff_hbm.at[:, :, pl.ds(part * quarter, quarter)],
            stiff_ref.at[:, :, pl.ds(part * quarter, quarter)],
            stiff_sems.at[part],
        )
        for part in range(4)
    ]
    for copy in small[:4] + big + small[4:]:
        copy.start()
    for copy in small[:4]:
        copy.wait()

    flags = flags_ref[...]
    flags_f = flags.astype(jnp.float32)
    tri = (
        lax.broadcasted_iota(jnp.int32, (128, 128), 0)
        <= lax.broadcasted_iota(jnp.int32, (128, 128), 1)
    ).astype(jnp.float32)
    inside = jnp.dot(flags_f, tri, preferred_element_type=jnp.float32)
    before = (
        lax.broadcasted_iota(jnp.int32, (32, 32), 1) < lax.broadcasted_iota(jnp.int32, (32, 32), 0)
    ).astype(jnp.float32)
    ahead = jnp.sum(
        jnp.dot(before, flags_f, preferred_element_type=jnp.float32), axis=1, keepdims=True
    )
    rank = jnp.where(flags == 1, (inside + ahead - 1.0).astype(jnp.int32), -1)
    rank_ref[...] = rank
    live_total = jnp.sum(flags_f)
    slot_rows = lax.broadcasted_iota(jnp.int32, (32, 128), 0)
    for row in range(32):
        picked = jnp.broadcast_to(rank_ref[row : row + 1, :], (32, 128)) == slot_rows
        sel_ref[row] = jnp.where(picked, 1.0, 0.0).astype(jnp.bfloat16)

    basis_ref[168:256, :] = jnp.zeros((88, 128), jnp.float32)

    def chunk_step(chunk, carry):
        lanes = lanes_of(chunk)
        names = nbr_ref[:, lanes]
        own = lax.broadcasted_iota(jnp.int32, (8, 128), 1) + chunk * 128
        mask = jnp.where(names != own, 1.0, 0.0)
        n0, n1, n2 = (nrm_ref[axis_id, :, lanes] for axis_id in range(3))
        length = br_ref[:, lanes]
        proj = [n0 * n0, n1 * n1, n2 * n2, n1 * n2, n0 * n2, n0 * n1]
        scaled = [length * value for value in proj]
        for comp in range(6):
            lp_ref[comp, :, lanes] = scaled[comp]
        for place, (row_id, col_id) in enumerate(PAIRS):
            basis_ref[place * 8 : (place + 1) * 8, :] = scaled[row_id] * scaled[col_id]
        for contact in range(CONTACTS):
            basis = basis_ref[pl.ds(contact, 32, stride=8), :]
            high = basis.astype(jnp.bfloat16)
            low = (basis - high.astype(jnp.float32)).astype(jnp.bfloat16)
            split_ref[contact * CHUNKS + chunk, 0:32, :] = high
            split_ref[contact * CHUNKS + chunk, 32:64, :] = low
        for slot in range(SLOT_COUNT):
            raw_ref[slot * 8 : (slot + 1) * 8, :] = (
                stiff_ref[slot, :, lanes].astype(jnp.float32) * mask
            )
        for group in range(GROUPS):
            total = None
            for contact in range(CONTACTS):
                value = raw_ref[pl.ds(group * 64 + contact, 8, stride=8), :]
                wt_ref[contact, group * 8 : (group + 1) * 8, lanes] = value
                total = value if total is None else total + value
            cd_ref[group * 8 : (group + 1) * 8, lanes] = RELAX_FACTOR / total
        return carry

    for part in range(4):
        big[part].wait()
        lax.fori_loop(part * CHUNKS // 4, (part + 1) * CHUNKS // 4, chunk_step, 0)

    acc = jnp.zeros((64, 32), jnp.float32)
    for contact in range(CONTACTS):
        weights = wt_ref[contact].astype(jnp.bfloat16)
        acc = acc + lax.dot_general(
            jnp.concatenate([split_ref[contact * CHUNKS + chunk] for chunk in range(CHUNKS)], axis=1),
            weights,
            NT,
            preferred_element_type=jnp.float32,
        )
    acc = acc[0:32] + acc[32:64]
    slot_lane = lax.broadcasted_iota(jnp.int32, (32, 32), 1).astype(jnp.float32)
    acc = jnp.where(slot_lane < live_total, acc * (1.0 / GRAINS), 0.0)
    tan_ref[...] = acc[:21]
    for copy in small[4:]:
        copy.wait()


def lerp(low_value, high_value, bit):
    weight = HIGH if bit else LOW
    return low_value + weight * (high_value - low_value)


def strain_rows(plane_refs, dup_ref):
    row = lax.broadcasted_iota(jnp.int32, (8, 128), 0)
    lane = lax.broadcasted_iota(jnp.int32, (8, 128), 1)
    z_weight = jnp.where(row < 4, LOW, HIGH)
    last_y = (row & 3) == 3
    last_z = lane == 127
    gradient = {}
    for axis_id in range(3):
        along, slope = {}, {}
        for bit_x in range(2):
            plane = plane_refs[bit_x][axis_id]
            dup_ref[0:4, :] = plane
            dup_ref[4:8, :] = plane
            base = dup_ref[...]
            for bit_y in range(2):
                value = base if bit_y == 0 else jnp.where(last_y, 0.0, pltpu.roll(base, 7, 0))
                after = jnp.where(last_z, 0.0, pltpu.roll(value, 127, 1))
                slope[bit_x, bit_y] = after - value
                along[bit_x, bit_y] = value + z_weight * (after - value)
        for gauss_y in range(2):
            for gauss_x in range(2):
                point = 2 * gauss_x + gauss_y
                face = [lerp(along[bit_x, 0], along[bit_x, 1], gauss_y) for bit_x in range(2)]
                gradient[point, axis_id, 0] = face[1] - face[0]
                gradient[point, axis_id, 1] = lerp(
                    along[0, 1] - along[0, 0], along[1, 1] - along[1, 0], gauss_x
                )
                edge = [lerp(slope[bit_x, 0], slope[bit_x, 1], gauss_y) for bit_x in range(2)]
                gradient[point, axis_id, 2] = lerp(edge[0], edge[1], gauss_x)
    return [
        [
            gradient[point, 0, 0],
            gradient[point, 1, 1],
            gradient[point, 2, 2],
            gradient[point, 1, 2] + gradient[point, 2, 1],
            gradient[point, 0, 2] + gradient[point, 2, 0],
            gradient[point, 0, 1] + gradient[point, 1, 0],
        ]
        for point in range(4)
    ]


def weigh(low_value, high_value, corner_bit):
    if corner_bit:
        return LOW * low_value + HIGH * high_value
    return HIGH * low_value + LOW * high_value


def force_rows(stress):
    row = lax.broadcasted_iota(jnp.int32, (8, 128), 0)
    lane = lax.broadcasted_iota(jnp.int32, (8, 128), 1)
    z_high = jnp.where(row < 4, LOW, HIGH)
    z_low = jnp.where(row < 4, HIGH, LOW)
    voigt = [[0, 5, 4], [5, 1, 3], [4, 3, 2]]
    planes = [[None] * 3, [None] * 3]
    for axis_id in range(3):
        part = [[stress[point][voigt[axis_id][other]] for point in range(4)] for other in range(3)]
        flow = [part[0][gauss_y] + part[0][2 + gauss_y] for gauss_y in range(2)]
        for bit_x in range(2):
            side_y = [weigh(part[1][gauss_y], part[1][2 + gauss_y], bit_x) for gauss_y in range(2)]
            side_z = [weigh(part[2][gauss_y], part[2][2 + gauss_y], bit_x) for gauss_y in range(2)]
            total_y = side_y[0] + side_y[1]
            total = None
            for bit_y in range(2):
                first = weigh(flow[0], flow[1], bit_y)
                first = first if bit_x else -first
                first = first + total_y if bit_y else first - total_y
                second = weigh(side_z[0], side_z[1], bit_y)
                near = z_low * first - second
                far = z_high * first + second
                far = jnp.where(lane == 0, 0.0, pltpu.roll(far, 1, 1))
                both = near + far
                both = both + pltpu.roll(both, 4, 0)
                if bit_y:
                    both = jnp.where((row & 3) == 0, 0.0, pltpu.roll(both, 1, 0))
                total = both if total is None else total + both
            planes[bit_x][axis_id] = 0.125 * total
    return planes


def relax_kernel(
    disp_ref,
    upper_ref,
    tangent_ref,
    rank_ref,
    sel_ref,
    wt_ref,
    cd_ref,
    lp_ref,
    nrm_ref,
    nbr_ref,
    tan_ref,
    carried_ref,
    stress_ref,
    band_ref,
    dup_ref,
    strain_ref,
    split_high_ref,
    split_low_ref,
    first_ref,
    fluct_a_ref,
    fluct_b_ref,
    sums_ref,
    onehot_ref,
    moved_ref,
    names_ref,
    near_ref,
):
    near_total = 0
    for chunk in range(CHUNKS):
        reach = (nbr_ref[:, chunk * 128 : (chunk + 1) * 128] - (chunk * 128 - 64)) & (GRAINS - 1)
        near_one = (jnp.max(reach.astype(jnp.float32)) < 256.0).astype(jnp.int32)
        near_ref[chunk] = near_one
        near_total = near_total + near_one
    all_near = near_total == CHUNKS

    tiles = strain_rows((disp_ref, upper_ref), dup_ref)
    for point in range(4):
        for comp in range(6):
            start = comp * 32 + point * 8
            strain_ref[start : start + 8, :] = tiles[point][comp]
    strain_ref[192:256, :] = jnp.zeros((64, 128), jnp.float32)

    for row in range(32):
        value = strain_ref[pl.ds(row, 8, stride=32), :]
        high = value.astype(jnp.bfloat16)
        split_high_ref[:, row * 128 : (row + 1) * 128] = high
        split_low_ref[:, row * 128 : (row + 1) * 128] = (value - high.astype(jnp.float32)).astype(
            jnp.bfloat16
        )
    sel = jnp.concatenate([sel_ref[row] for row in range(32)], axis=1)
    slot_strain = lax.dot_general(
        sel, split_high_ref[...], NT, preferred_element_type=jnp.float32
    ) + lax.dot_general(sel, split_low_ref[...], NT, preferred_element_type=jnp.float32)
    columns = [
        [
            jnp.broadcast_to(slot_strain[group * 8 : (group + 1) * 8, comp : comp + 1], (8, 128))
            for comp in range(6)
        ]
        for group in range(GROUPS)
    ]
    strain_table = jnp.zeros((32, 128), jnp.float32)
    strain_lane = lax.broadcasted_iota(jnp.int32, (32, 128), 1)
    for comp in range(6):
        strain_table = jnp.where(
            strain_lane == comp, slot_strain[:, comp : comp + 1], strain_table
        )
    strain_full = jnp.concatenate([strain_table, jnp.zeros((96, 128), jnp.float32)], axis=0)
    strain_t = jnp.transpose(strain_full)[0:8, 0:32]
    sums_ref[...] = jnp.zeros((192, 128), jnp.float32)

    def first_step(chunk, carry):
        lanes = lanes_of(chunk)
        block = lax.broadcasted_iota(jnp.int32, (16, 128), 0).astype(jnp.float32)
        for contact in range(CONTACTS):
            names = jnp.broadcast_to(nbr_ref[contact : contact + 1, lanes], (16, 128))
            wanted = (names & 127) + jnp.where((names >> 7) == chunk, 0, 128)
            wanted = (wanted.astype(jnp.float32) - block).astype(jnp.bfloat16)
            onehot_ref[chunk * CONTACTS + contact] = jnp.concatenate(
                [
                    jnp.where(wanted == jnp.bfloat16(part * 16), jnp.bfloat16(1), jnp.bfloat16(0))
                    for part in range(16)
                ],
                axis=0,
            )
        for pair in range(0, GROUPS, 2):
            groups = (pair, pair + 1)
            totals = {}
            for contact in range(CONTACTS):
                basis = [row8(lp_ref.at[comp], contact, lanes) for comp in range(6)]
                normal = [row8(nrm_ref.at[axis_id], contact, lanes) for axis_id in range(3)]
                for group in groups:
                    rows = slice(group * 8, (group + 1) * 8)
                    affine = columns[group][0] * basis[0]
                    for comp in range(1, 6):
                        affine = affine + columns[group][comp] * basis[comp]
                    force = wt_ref[contact, rows, lanes] * affine
                    for axis_id in range(3):
                        term = force * normal[axis_id]
                        key = (group, axis_id)
                        totals[key] = totals[key] + term if contact else term
            for group in groups:
                factor = cd_ref[group * 8 : (group + 1) * 8, lanes]
                for axis_id in range(3):
                    start = axis_id * 32 + group * 8
                    first_ref[start : start + 8, lanes] = factor * totals[group, axis_id]
        return carry

    lax.fori_loop(0, CHUNKS, first_step, 0)

    half = lax.broadcasted_iota(jnp.int32, (8, 128), 1) < 64

    def gather_near(source_ref, chunk, moved_ref):
        lanes = lanes_of(chunk)
        lanes_up = lanes_of((chunk + 1) & (CHUNKS - 1))
        lanes_down = lanes_of((chunk + CHUNKS - 1) & (CHUNKS - 1))
        tiles = [slice(tile * 8, (tile + 1) * 8) for tile in range(12)]
        own = [source_ref[tile, lanes] for tile in tiles]
        sides = [
            jnp.where(half, source_ref[tile, lanes_up], source_ref[tile, lanes_down])
            for tile in tiles
        ]
        for contact in range(CONTACTS):
            names = row8(nbr_ref, contact, lanes)
            index = names & 127
            inside = (names >> 7) == chunk
            for place, tile in enumerate(tiles):
                moved_ref[tile, contact * 128 : (contact + 1) * 128] = jnp.where(
                    inside, take_lanes(own[place], index), take_lanes(sides[place], index)
                )

    tall = lax.broadcasted_iota(jnp.int32, (96, 128), 1) < 64

    def dot_pieces(source_ref, chunk, exact):
        lanes = lanes_of(chunk)
        lanes_up = lanes_of((chunk + 1) & (CHUNKS - 1))
        lanes_down = lanes_of((chunk + CHUNKS - 1) & (CHUNKS - 1))
        own = source_ref[:, lanes]
        sides = jnp.where(tall, source_ref[:, lanes_up], source_ref[:, lanes_down])
        window = jnp.concatenate([own, sides], axis=1)
        high = window.astype(jnp.bfloat16)
        if exact:
            low = (window - high.astype(jnp.float32)).astype(jnp.bfloat16)
            both = jnp.concatenate([high, low], axis=0)

        def pieces(pair):
            place = chunk * CONTACTS + 2 * pair
            picks = jnp.concatenate([onehot_ref[place], onehot_ref[place + 1]], axis=1)
            if not exact:
                return jnp.dot(high, picks, preferred_element_type=jnp.float32)
            value = jnp.dot(both, picks, preferred_element_type=jnp.float32)
            return value[0:96] + value[96:192]

        return pieces

    def scratch_pieces(moved_ref):
        return lambda pair: moved_ref[:, pair * 256 : (pair + 1) * 256]

    def chunk_forces(source_ref, chunk, pieces, use):
        lanes = lanes_of(chunk)
        own = [source_ref[tile * 8 : (tile + 1) * 8, lanes] for tile in range(12)]
        for pair in range(CONTACTS // 2):
            moved = pieces(pair)
            for half_id in range(2):
                contact = 2 * pair + half_id
                columns_of = slice(half_id * 128, (half_id + 1) * 128)
                normal = [row8(nrm_ref.at[axis_id], contact, lanes) for axis_id in range(3)]
                for group in range(GROUPS):
                    stretch = None
                    for axis_id in range(3):
                        tile = axis_id * 4 + group
                        there = moved[tile * 8 : (tile + 1) * 8, columns_of]
                        term = normal[axis_id] * (there - own[tile])
                        stretch = term if stretch is None else stretch + term
                    rows = slice(group * 8, (group + 1) * 8)
                    use(contact, group, wt_ref[contact, rows, lanes] * stretch, normal)
        return own

    def gather_far(source_ref, chunk, moved_ref):
        lanes = lanes_of(chunk)
        for contact in range(CONTACTS):
            names_ref[contact] = row8(nbr_ref, contact, lanes)

        def contact_step(contact, carry):
            names = names_ref[contact]
            index = names & 127
            block = names >> 7

            def step(place, values):
                hit = block == place
                return tuple(
                    jnp.where(
                        hit,
                        take_lanes(source_ref[tile * 8 : (tile + 1) * 8, lanes_of(place)], index),
                        values[tile],
                    )
                    for tile in range(12)
                )

            zero = jnp.zeros((8, 128), jnp.float32)
            values = lax.fori_loop(0, CHUNKS, step, (zero,) * 12)
            for tile in range(12):
                moved_ref[tile * 8 : (tile + 1) * 8, lanes_of(contact)] = values[tile]
            return carry

        lax.fori_loop(0, CONTACTS, contact_step, 0)

    def all_chunks(source_ref, work, exact):
        unroll = 4 if exact else 8

        @pl.when(all_near)
        def _():
            def step(turn, carry):
                for place in range(unroll):
                    chunk = turn * unroll + place
                    work(chunk, dot_pieces(source_ref, chunk, exact))
                return carry

            lax.fori_loop(0, CHUNKS // unroll, step, 0)

        @pl.when(jnp.logical_not(all_near))
        def _():
            def step(chunk, carry):
                near = near_ref[chunk] == 1

                @pl.when(near)
                def _():
                    gather_near(source_ref, chunk, moved_ref)

                @pl.when(jnp.logical_not(near))
                def _():
                    gather_far(source_ref, chunk, moved_ref)

                work(chunk, scratch_pieces(moved_ref))
                return carry

            lax.fori_loop(0, CHUNKS, step, 0)

    def sweep(source_ref, target_ref):
        def work(chunk, pieces):
            totals = [None] * 12

            def use(contact, group, force, normal):
                for axis_id in range(3):
                    tile = axis_id * 4 + group
                    term = force * normal[axis_id]
                    totals[tile] = totals[tile] + term if contact else term

            own = chunk_forces(source_ref, chunk, pieces, use)
            lanes = lanes_of(chunk)
            for group in range(GROUPS):
                factor = cd_ref[group * 8 : (group + 1) * 8, lanes]
                for axis_id in range(3):
                    tile = axis_id * 4 + group
                    rows = slice(tile * 8, (tile + 1) * 8)
                    target_ref[rows, lanes] = own[tile] + first_ref[rows, lanes] + factor * totals[tile]

        all_chunks(source_ref, work, EXACT)

    def stress_work(chunk, pieces):
        lanes = lanes_of(chunk)
        totals = [None] * 24

        def use(contact, group, force, normal):
            for comp in range(6):
                tile = comp * 4 + group
                term = force * row8(lp_ref.at[comp], contact, lanes)
                totals[tile] = totals[tile] + term if contact else term

        chunk_forces(current, chunk, pieces, use)
        for tile in range(24):
            sums_ref[tile * 8 : (tile + 1) * 8, :] += totals[tile]

    current = first_ref
    for turn in range(SWEEPS - 1):
        target = fluct_b_ref if turn % 2 else fluct_a_ref
        sweep(current, target)
        current = target
    all_chunks(current, stress_work, True)

    lane32 = lax.broadcasted_iota(jnp.int32, (32, 128), 1)
    table = jnp.zeros((32, 128), jnp.float32)
    for comp in range(6):
        total = jnp.sum(sums_ref[comp * 32 : (comp + 1) * 32, :], axis=1, keepdims=True)
        table = jnp.where(lane32 == comp, total * (1.0 / GRAINS), table)
    full = jnp.concatenate([table, jnp.zeros((96, 128), jnp.float32)], axis=0)
    shares = []
    for row_id in range(6):
        share = None
        for col_id in range(6):
            where = PAIRS.index((min(row_id, col_id), max(row_id, col_id)))
            term = tan_ref[where : where + 1, :] * strain_t[col_id : col_id + 1, :]
            share = term if share is None else share + term
        shares.append(share)
    flipped = jnp.transpose(full)[0:6, 0:32] + jnp.concatenate(shares, axis=0)
    band_ref[...] = flipped
    dup_ref[0:6, 0:32] = flipped

    strain = [strain_ref[comp * 32 : (comp + 1) * 32, :] for comp in range(6)]
    rank = rank_ref[...]
    banded = rank >= 0
    place = jnp.maximum(rank, 0)
    stress = []
    for row_id in range(6):
        running = None
        for col_id in range(6):
            where = PAIRS.index((min(row_id, col_id), max(row_id, col_id)))
            term = (
                tangent_ref[where * 32 : (where + 1) * 32, :].astype(jnp.float32) * strain[col_id]
            )
            running = term if running is None else running + term
        values = take_lanes(jnp.broadcast_to(dup_ref[row_id : row_id + 1, :], (32, 128)), place)
        value = jnp.where(banded, values, running)
        stress_ref[row_id * 32 : (row_id + 1) * 32, :] = value
        stress.append(value)
    planes = force_rows(tiles_of(stress))
    for axis_id in range(3):
        carried_ref[axis_id] = planes[1][axis_id][0:4]


def tiles_of(stress):
    return [
        [stress[comp][point * 8 : (point + 1) * 8, :] for comp in range(6)] for point in range(4)
    ]


def output_kernel(stress_in, band_in, tan_in, load_ref, pre_ref, stress_ref, band_ref, tan_ref):
    stress_ref[...] = stress_in[...]
    band_ref[...] = band_in[...]
    tan_ref[...] = tan_in[...]
    planes = force_rows(tiles_of([stress_in[comp * 32 : (comp + 1) * 32, :] for comp in range(6)]))
    for axis_id in range(3):
        pre_ref[axis_id] = load_ref[axis_id] - planes[0][axis_id][0:4]


VMEM = pl.BlockSpec(memory_space=pltpu.VMEM)
HBM = pl.BlockSpec(memory_space=pltpu.HBM)


def run_template(
    flags, stiffness, normals, branch_length, neighbours, displacement, load, elastic_tangent
):
    f32 = jnp.float32
    kept = [normals, neighbours, displacement, load, elastic_tangent]
    return pl.pallas_call(
        template_kernel,
        out_shape=(
            jax.ShapeDtypeStruct((CONTACTS, SLOT_COUNT, GRAINS), f32),
            jax.ShapeDtypeStruct((SLOT_COUNT, GRAINS), f32),
            jax.ShapeDtypeStruct((21, SLOT_COUNT), f32),
            jax.ShapeDtypeStruct((32, 128), jnp.int32),
            jax.ShapeDtypeStruct((32, SLOT_COUNT, 128), jnp.bfloat16),
            jax.ShapeDtypeStruct((6, CONTACTS, GRAINS), f32),
        )
        + tuple(jax.ShapeDtypeStruct(value.shape, value.dtype) for value in kept),
        in_specs=[HBM] * 8,
        out_specs=(VMEM,) * 11,
        scratch_shapes=[
            pltpu.VMEM((SLOT_COUNT * CONTACTS, 128), f32),
            pltpu.VMEM((256, 128), f32),
            pltpu.VMEM((CONTACTS * CHUNKS, 64, 128), jnp.bfloat16),
            pltpu.VMEM((32, 128), jnp.int32),
            pltpu.VMEM((SLOT_COUNT, CONTACTS, GRAINS), jnp.bfloat16),
            pltpu.VMEM((CONTACTS, GRAINS), f32),
            pltpu.SemaphoreType.DMA((7,)),
            pltpu.SemaphoreType.DMA((4,)),
        ],
        cost_estimate=pl.CostEstimate(flops=40_000_000, bytes_accessed=8_000_000, transcendentals=0),
        compiler_params=pltpu.CompilerParams(vmem_limit_bytes=16 * 1024 * 1024),
        name="template",
    )(
        *[
            pltpu.with_memory_space_constraint(value, pltpu.HBM)
            for value in (flags, stiffness, *kept[:1], branch_length, *kept[1:])
        ]
    )


def run_relax(disp, upper, tangent, rank, sel, wt, cd, lp, normals, neighbours, tan):
    f32 = jnp.float32
    return pl.pallas_call(
        relax_kernel,
        out_shape=(
            jax.ShapeDtypeStruct((3, 4, 128), f32),
            jax.ShapeDtypeStruct((192, 128), f32),
            jax.ShapeDtypeStruct((6, SLOT_COUNT), f32),
        ),
        in_specs=[VMEM] * 11,
        out_specs=(VMEM,) * 3,
        scratch_shapes=[
            pltpu.VMEM((8, 128), f32),
            pltpu.VMEM((256, 128), f32),
            pltpu.VMEM((8, 4096), jnp.bfloat16),
            pltpu.VMEM((8, 4096), jnp.bfloat16),
            pltpu.VMEM((96, GRAINS), f32),
            pltpu.VMEM((96, GRAINS), f32),
            pltpu.VMEM((96, GRAINS), f32),
            pltpu.VMEM((192, 128), f32),
            pltpu.VMEM((CHUNKS * CONTACTS, 256, 128), jnp.bfloat16),
            pltpu.VMEM((96, CONTACTS * 128), f32),
            pltpu.VMEM((CONTACTS, 8, 128), jnp.int32),
            pltpu.SMEM((CHUNKS,), jnp.int32),
        ],
        cost_estimate=pl.CostEstimate(
            flops=200_000_000, bytes_accessed=8_000_000, transcendentals=0
        ),
        compiler_params=pltpu.CompilerParams(vmem_limit_bytes=28 * 1024 * 1024),
        name="relax",
    )(disp, upper, tangent, rank, sel, wt, cd, lp, normals, neighbours, tan)


def run_output(stress, band, tan, load):
    f32 = jnp.float32
    return pl.pallas_call(
        output_kernel,
        out_shape=(
            jax.ShapeDtypeStruct((3, 4, 128), f32),
            jax.ShapeDtypeStruct((192, 128), f32),
            jax.ShapeDtypeStruct((6, SLOT_COUNT), f32),
            jax.ShapeDtypeStruct((21, SLOT_COUNT), f32),
        ),
        in_specs=[VMEM] * 4,
        out_specs=(VMEM,) * 4,
        cost_estimate=pl.CostEstimate(flops=1_000_000, bytes_accessed=2_000_000, transcendentals=0),
        compiler_params=pltpu.CompilerParams(vmem_limit_bytes=8 * 1024 * 1024),
        name="output",
    )(stress, band, tan, load)


def body(
    displacement,
    load,
    elastic_tangent,
    band_flags,
    contact_stiffness,
    normals,
    branch_length,
    neighbours,
):
    upper = shifted(displacement, ("row", "col"), -1)
    wt, cd, tan, rank, sel, lp, nrm, nbr, disp, load_here, elastic = run_template(
        band_flags.reshape(32, 128),
        contact_stiffness,
        normals,
        branch_length,
        neighbours,
        displacement.reshape(3, 4, 128),
        load.reshape(3, 4, 128),
        elastic_tangent.reshape(672, 128),
    )
    carried, stress_here, band_here = run_relax(
        disp, upper.reshape(3, 4, 128), elastic, rank, sel, wt, cd, lp, nrm, nbr, tan
    )
    arrived = shifted(carried, ("row", "col"), 1)
    pre, stress, band, tangent = run_output(stress_here, band_here, tan, load_here)
    residual = (pre - arrived).reshape(3, 1, 4, 128)
    return (residual, stress.reshape(6, 8, 1, 4, 128), tangent, band)


def solution(mesh):
    placed = (
        P(None, ("row", "col"), None, None),
        P(None, ("row", "col"), None, None),
        P(None, None, ("row", "col"), None, None),
        P(None, ("row", "col"), None, None),
        P(("row", "col"), None, None),
        P(),
        P(),
        P(),
    )
    return jax.shard_map(
        body,
        mesh=mesh,
        in_specs=placed,
        out_specs=(
            P(None, ("row", "col"), None, None),
            P(None, None, ("row", "col"), None, None),
            P(None, ("row", "col")),
            P(None, ("row", "col")),
        ),
        check_vma=False,
    )
```
